256 devices in a mesh: seq: 8 (over z_hi, core), expert: 16 (over y, x), tensor: 2 (over z_lo).
Axes of the slice: x: 4, y: 4, z: 8 (z_hi: 4, z_lo: 2; z = z_hi * 2 + z_lo), core: 2. Of those that a mesh axis runs over, the one named last changes fastest.
Arguments:
- q_rows: bfloat16 [16, 1024, 4096], P('expert', 'seq', 'tensor'), may hold values from -6 to 6
- k_rows: bfloat16 [16, 1024, 512], P('expert', 'seq', 'tensor'), may hold values from -6 to 6
- value_rows: bfloat16 [16, 1024, 512], P('expert', 'seq', 'tensor'), may hold values from -6 to 6
- x_rows: bfloat16 [16, 1024, 2048], P('expert', 'seq'), may hold values from -40 to 40
- out_weight: bfloat16 [4096, 2048], P('tensor', 'expert'), may hold values from -0.09375 to 0.09375
- norm_gain: float32 [2048], P('tensor'), may hold values from 0.1 to 1.9
- w_gate: bfloat16 [128, 2048, 768], P(('seq', 'expert'), None, 'tensor'), may hold values from -0.125 to 0.125
- w_up: bfloat16 [128, 2048, 768], P(('seq', 'expert'), None, 'tensor'), may hold values from -0.125 to 0.125
- w_down: bfloat16 [128, 768, 2048], P(('seq', 'expert'), 'tensor'), may hold values from -0.21875 to 0.21875
- expert_ids: int32 [16, 1024, 8], P('expert', 'seq'), may hold values from 0 to 127, all different within a row; in each aligned block of 128 rows (0 to 127, 128 to 255, ..., all dimensions but the last counted through in order) at most 12 rows name the same one
- gate_weights: float32 [16, 1024, 8], P('expert', 'seq'), may hold values from 0.02 to 0.4
Outputs:
- layer_out: bfloat16 [16, 1024, 2048], P('expert', 'seq', 'tensor')
The draws below stay inside these ranges and needn't reach their ends.
Inputs may be any that keep to these rules, and one draw needn't show every extreme that they name: `expert_ids`: in each token's row the 8 ids differ. Among the 128 tokens of one block of positions (the blocks laid session after session) no expert is named more than 12 times, a bound that some block reaches; every expert is named somewhere.
All inputs are finite; a program needn't handle non-finite values.
Results may differ from the reference program's by a relative error of at most 0.007.
Values may be sent and summed in bfloat16 or wider, within the bound.
A program may use at most 128 MiB of HBM per device.

```python
import math
import jax
import jax.numpy as jnp
import numpy as np
from jax import lax

D = 2048
QUERY_HEADS = 32
KEY_VALUE_HEADS = 4
HEAD_SIZE = 128
FF = 768
TOPK = 8
TOK_DEV = 128
EXPERTS = 128
SESSION_COUNT = 16
SESSION_LENGTH = 1024
CAP = 12
N_TENSOR = 2


def draw_q_rows(key, part):
    random_key = jax.random.fold_in(key, 1)
    base_rows = jnp.clip(1.7 * jax.random.normal(random_key, (SESSION_COUNT, SESSION_LENGTH, QUERY_HEADS * HEAD_SIZE), jnp.float32), -6.0, 6.0)
    return base_rows.astype(jnp.bfloat16)


def draw_k_rows(key, part):
    random_key = jax.random.fold_in(key, 2)
    base_rows = jnp.clip(1.7 * jax.random.normal(random_key, (SESSION_COUNT, SESSION_LENGTH, KEY_VALUE_HEADS * HEAD_SIZE), jnp.float32), -6.0, 6.0)
    return base_rows.astype(jnp.bfloat16)


def draw_x_rows(key, part):
    random_key = jax.random.fold_in(key, 3)
    row_key = jax.random.fold_in(key, 4)
    column_key = jax.random.fold_in(key, 5)
    spread = 1.15
    base_rows = jnp.clip(jax.random.normal(random_key, (SESSION_COUNT, SESSION_LENGTH, D), jnp.float32), -4.0, 4.0)
    row_scale = jnp.exp(jax.random.uniform(row_key, (SESSION_COUNT, SESSION_LENGTH, 1), jnp.float32, -spread, spread))
    column_scale = jnp.exp(jax.random.uniform(column_key, (1, 1, D), jnp.float32, -spread, spread))
    return (base_rows * row_scale * column_scale).astype(jnp.bfloat16)


def block_scale(key, extent, cuts, least, high):
    loudness = 1.0
    for position, shards_of in cuts:
        draws = jax.random.uniform(jax.random.fold_in(jax.random.fold_in(key, 6), position), (shards_of,), jnp.float32, least / len(cuts), high / len(cuts))
        loudness = loudness * jnp.repeat(jnp.exp(draws), extent[position] // shards_of).reshape((-1,) + (1,) * (len(extent) - 1 - position))
    return loudness


def deal_out(rng, own, number, rows, number_of, top, limit, slope):
    ranking = jax.random.permutation(rng, number_of)
    crowded, common = load_shares(number_of, rows * top, limit, slope, True), load_shares(number_of, rows * top, limit, slope, False)
    places = jnp.arange(number_of)

    def named(sizes, rotation):
        used = int((sizes > 0).sum())
        fixed = max(1, used // 4)
        passed = fixed + (places - fixed + rotation * (used - fixed)) % max(1, number_of - fixed)
        return jnp.zeros((number_of,), jnp.int32).at[ranking[jnp.where(places < fixed, places, passed)]].set(jnp.asarray(sizes, jnp.int32))

    sizes = jnp.where(number % 4 == 0, named(crowded, number // 4), named(common, number - number // 4 - 1))
    mixed = jax.random.permutation(jax.random.fold_in(own, 3), number_of)
    giver, sink = mixed[0:number_of // 2 * 2:2], mixed[1:number_of // 2 * 2:2]
    margin = jnp.minimum(sizes[giver] - 1, limit - sizes[sink]) // 2
    margin = jnp.where((giver == ranking[0]) | (sink == ranking[0]) | (sizes[sink] == 0), 0, jnp.maximum(margin, 0))
    passed = jax.random.randint(jax.random.fold_in(own, 4), (number_of // 2,), 0, 1 << 20) % (margin + 1)
    sizes = sizes.at[giver].add(-passed).at[sink].add(passed)
    members = jnp.searchsorted(jnp.cumsum(sizes), jnp.arange(rows * top), side="right").astype(jnp.int32)
    listing = members.reshape(top, rows).T
    listing = listing[jax.random.permutation(jax.random.fold_in(own, 1), rows)]
    rotation = jax.random.randint(jax.random.fold_in(own, 2), (rows, 1), 0, top)
    return jnp.take_along_axis(listing, (jnp.arange(top)[None, :] + rotation) % top, axis=1)


def load_shares(count, total, limit, skew, full):
    weights = [(1 << 20) // math.isqrt(grade ** skew) + 1 for grade in range(1, count + 1)]
    largest = limit if full else min(limit, max(-(-total // count), total * weights[0] // sum(weights)))
    least = 1 if total - largest >= count - 1 else 0
    holding, rest = [largest] + [least] * (count - 1), total - largest - least * (count - 1)
    while rest > 0:
        free = [i for i in range(1, count) if holding[i] < largest] or [i for i in range(1, count) if holding[i] < limit]
        pool, remaining = sum([weights[i] for i in free]), rest
        for i in free:
            addition = min(limit - holding[i], max(1, remaining * weights[i] // pool), rest)
            holding[i] = holding[i] + addition
            rest = rest - addition
    return np.array(holding)


def scatter_about(rng, shape, scale, most, pieces=(), kind=jnp.bfloat16):
    entries = jax.random.normal(rng, shape, jnp.float32) * scale
    if len(pieces) > 0:
        entries = block_scale(rng, shape, pieces, -0.22, 0.18) * entries
    return jnp.clip(entries, min=-most, max=most).astype(kind)


def setup_inputs(seed: int = 0) -> dict:
    keys = jax.random.split(jax.random.key(seed), 12)
    q_rows = draw_q_rows(jax.random.fold_in(keys[11], 71), 0)
    k_rows = draw_k_rows(jax.random.fold_in(keys[11], 71), 0)
    value_rows = scatter_about(keys[2], (SESSION_COUNT, SESSION_LENGTH, KEY_VALUE_HEADS * HEAD_SIZE), 1.0, 6.0, ((0, 16), (1, 8), (2, 2)))
    x_rows = draw_x_rows(jax.random.fold_in(keys[11], 71), 0)
    out_weight = scatter_about(keys[4], (QUERY_HEADS * HEAD_SIZE, D), (QUERY_HEADS * HEAD_SIZE) ** -0.5, 0.09375, ((0, 2), (1, 16)))
    norm_gain = jnp.clip(1.0 + 0.18 * jax.random.normal(keys[5], (D,), jnp.float32), 0.1, 1.9)
    w_gate = scatter_about(keys[6], (EXPERTS, D, FF), D ** -0.5, 0.125, ((0, 128), (2, 2)))
    w_up = scatter_about(keys[7], (EXPERTS, D, FF), D ** -0.5, 0.125, ((0, 128), (2, 2)))
    w_down = scatter_about(keys[8], (EXPERTS, FF, D), FF ** -0.5, 0.21875, ((0, 128), (1, 2)))
    expert_ids_keys = jax.random.split(jax.random.fold_in(keys[9], 1), SESSION_COUNT * SESSION_LENGTH // TOK_DEV)
    expert_ids_turns = jax.random.permutation(jax.random.fold_in(keys[9], 3), SESSION_COUNT * SESSION_LENGTH // TOK_DEV)
    expert_ids = jax.vmap(lambda own, number: deal_out(jax.random.fold_in(keys[9], 2), own, number, TOK_DEV, EXPERTS, TOPK, CAP, 2))(expert_ids_keys, expert_ids_turns).reshape((SESSION_COUNT, SESSION_LENGTH, TOPK))
    gate_weights = jnp.clip(0.02 + 0.38 * jax.random.uniform(keys[10], (SESSION_COUNT, SESSION_LENGTH, TOPK), jnp.float32) ** block_scale(keys[10], (SESSION_COUNT, SESSION_LENGTH, TOPK), ((0, 16), (1, 8)), -0.2, 0.2), 0.02, 0.4)
    return {"q_rows": q_rows, "k_rows": k_rows, "value_rows": value_rows, "x_rows": x_rows, "out_weight": out_weight, "norm_gain": norm_gain, "w_gate": w_gate, "w_up": w_up, "w_down": w_down, "expert_ids": expert_ids, "gate_weights": gate_weights}


def rounded(value):
    return lax.optimization_barrier(value.astype(jnp.bfloat16)).astype(jnp.float32)

def attend_session(query_session, key_session, value_session):
    group_width = QUERY_HEADS // KEY_VALUE_HEADS
    query_float = query_session.astype(jnp.float32).reshape(SESSION_LENGTH, KEY_VALUE_HEADS, group_width, HEAD_SIZE)
    key_float = key_session.astype(jnp.float32).reshape(SESSION_LENGTH, KEY_VALUE_HEADS, HEAD_SIZE)
    value_float = value_session.astype(jnp.float32).reshape(SESSION_LENGTH, KEY_VALUE_HEADS, HEAD_SIZE)
    scores = jnp.einsum('igrd,jgd->grij', query_float, key_float, precision=lax.Precision.HIGHEST) * (1.0 / math.sqrt(HEAD_SIZE))
    places = jnp.arange(SESSION_LENGTH, dtype=jnp.int32)
    allowed = places[None, :] <= places[:, None]
    scores = jnp.where(allowed, scores, -jnp.inf)
    row_max = lax.optimization_barrier(jnp.max(scores, axis=-1, keepdims=True))
    weights = jnp.where(allowed, jnp.exp(scores - row_max), jnp.float32(0.0))
    totals = lax.optimization_barrier(jnp.sum(weights, axis=-1))
    summed = jnp.einsum('grij,jgd->igrd', rounded(weights), value_float, precision=lax.Precision.HIGHEST)
    result = summed / jnp.transpose(totals, (2, 0, 1))[..., None]
    return result.reshape(SESSION_LENGTH, QUERY_HEADS * HEAD_SIZE).astype(jnp.bfloat16)

def reference(q_rows, k_rows, value_rows, x_rows, out_weight, norm_gain, w_gate, w_up, w_down, expert_ids, gate_weights):
    attn_rows = lax.map(lambda items: attend_session(items[0], items[1], items[2]), (q_rows, k_rows, value_rows))
    all_tokens = SESSION_COUNT * SESSION_LENGTH
    flat_attn = attn_rows.reshape(all_tokens, QUERY_HEADS * HEAD_SIZE)
    head_width = QUERY_HEADS * HEAD_SIZE // N_TENSOR
    projected = jnp.zeros((all_tokens, D), jnp.float32)
    for group_pos in range(N_TENSOR):
        lo_col = group_pos * head_width
        piece = jnp.dot(flat_attn[:, lo_col:lo_col + head_width], out_weight[lo_col:lo_col + head_width], preferred_element_type=jnp.float32)
        projected = projected + rounded(piece)
    mixed = x_rows.reshape(all_tokens, D).astype(jnp.float32) + projected
    inverse = lax.rsqrt(lax.optimization_barrier(jnp.mean(mixed * mixed, axis=1)) + 1e-06)
    normed = (mixed * inverse[:, None] * norm_gain.astype(jnp.float32)[None, :]).astype(jnp.bfloat16)
    blocks = all_tokens // TOK_DEV
    per_block = TOK_DEV * TOPK
    routed = expert_ids.reshape(blocks, per_block)
    member = (routed[:, :, None] == jnp.arange(EXPERTS, dtype=jnp.int32)[None, None, :]).astype(jnp.int32)
    earlier = jnp.cumsum(member, axis=1) - member
    slot_index = lax.optimization_barrier(jnp.sum(earlier * member, axis=2))
    block_index = jnp.arange(blocks, dtype=jnp.int32)[:, None]
    target = (routed * blocks + block_index) * CAP + slot_index
    token_index = block_index * TOK_DEV + jnp.arange(per_block, dtype=jnp.int32)[None, :] // TOPK
    table = jnp.full((EXPERTS * blocks * CAP,), all_tokens, jnp.int32)
    table = table.at[target.reshape(-1)].set(token_index.reshape(-1).astype(jnp.int32)).reshape(EXPERTS, blocks * CAP)
    gate_table = jnp.zeros((EXPERTS * blocks * CAP,), jnp.float32)
    gate_table = gate_table.at[target.reshape(-1)].set(gate_weights.reshape(-1).astype(jnp.float32)).reshape(EXPERTS, blocks * CAP)
    padded = jnp.concatenate([normed, jnp.zeros((1, D), jnp.bfloat16)], axis=0)
    hidden_width = FF // N_TENSOR

    def expert_step(carry, items):
        rows_of, gates_of, gate_w, up_w, down_w = items
        rows = padded[rows_of]
        gate_act = jnp.dot(rows, gate_w, preferred_element_type=jnp.float32)
        up_act = jnp.dot(rows, up_w, preferred_element_type=jnp.float32)
        hidden = (jax.nn.silu(gate_act) * up_act).astype(jnp.bfloat16)
        expert_sum = jnp.zeros((rows.shape[0], D), jnp.float32)
        for group_pos in range(N_TENSOR):
            lo_col = group_pos * hidden_width
            piece = jnp.dot(hidden[:, lo_col:lo_col + hidden_width], down_w[lo_col:lo_col + hidden_width], preferred_element_type=jnp.float32)
            expert_sum = expert_sum + rounded(piece)
        expert_out = expert_sum.astype(jnp.bfloat16).astype(jnp.float32)
        carry = carry.at[rows_of].add(gates_of[:, None] * expert_out)
        return (carry, None)
    starting = jnp.zeros((all_tokens + 1, D), jnp.float32)
    blended, unused = lax.scan(expert_step, starting, (table, gate_table, w_gate, w_up, w_down))
    layer_out = (mixed + blended[:all_tokens]).astype(jnp.bfloat16)
    return layer_out.reshape(SESSION_COUNT, SESSION_LENGTH, D)
```

```python
import math

import jax
import jax.numpy as jnp
from jax import lax
from jax.experimental import pallas as pl
from jax.experimental.pallas import tpu as pltpu
from jax.sharding import PartitionSpec as P

MESH = pl.DeviceIdType.MESH
BF = jnp.bfloat16
F32 = jnp.float32

NX, NY, NZ = 4, 4, 8
NP = NX * NY
HEAD = 128
TOK = 128
HALF_TOK = 64
D = 2048
CAP = 12
NBLK = 4
MSG = NBLK * CAP
ROWS = NP * MSG
TOKS = NBLK * TOK
NF = 4
FC = D // NF
FFH = 384
FF = 768
HALF_D = D // 2
WROWS = 1024
ORDER = (0, 2, 1, 3)


def layer_kernel(
    q_h, k_h, v_h, x_h, w_h, gain_h, wg_h, wu_h, wd_h, ids_h, gat_h,
    out_ref,
    q_v, x_v, kv_v, w_v, gain_v, ids_v, gat_v,
    attn_v, ph_v, px_v, px2_v, mix_v, mixo_v,
    xg_v, p_v, gt_v, g_v, s_v, r_v,
    wg_v, wu_v, wd_v, ag_v, au_v, hid_v,
    y_v, yr_v, o_v, rs_s, rs_r,
    loc, hk, hz, wz_s, wk_s, wf_s,
    kv_s, kv_r, kvc_s, kvc_r, kv2_s, kv2_r,
    sm_s, sm_r,
    wa_s, wa_r, wa2_r, wb_s, wb_r, wb2_r, wc_s, wc_r,
    px_s, px_r, px2_s, px2_r,
    xg_s, xg_r, dsp_s, dsp_r, dsp_l, ret_s, ret_r, ret_l,
    rs_ss, rs_rs,
):
    rem, div = lax.rem, lax.div
    s = lax.axis_index("seq")
    e = lax.axis_index("expert")
    t = lax.axis_index("tensor")
    zh = div(s, 2)
    c = rem(s, 2)
    z = zh * 2 + t
    y = div(e, NX)
    x = rem(e, NX)
    oc = 1 - c
    giver = rem(c + t, 2)

    def dev(zz, ee, cc):
        return (div(zz, 2) * 2 + cc, ee, rem(zz, 2))

    def zmod(v):
        return rem(v + NZ, NZ)

    def send(src, dst, ss, rs, who):
        cp = pltpu.make_async_remote_copy(
            src_ref=src, dst_ref=dst, send_sem=ss, recv_sem=rs, device_id=who, device_id_type=MESH
        )
        cp.start()

    def local(src, dst, sem):
        pltpu.make_async_copy(src, dst, sem).start()

    def wait(ref, sem):
        pltpu.make_async_copy(ref, ref, sem).wait()

    def m8(v, n):
        return pl.multiple_of(v, n)

    other = dev(z, e, oc)
    partner = dev(z + 1 - 2 * t, e, c)
    cross = dev(z + 1 - 2 * t, e, oc)
    z_next, z_prev = dev(zmod(z + 1), e, c), dev(zmod(z - 1), e, c)
    zh_next, zh_prev = dev(zmod(z + 2), e, c), dev(zmod(z - 2), e, c)
    zh_opp = dev(zmod(z + 4), e, c)

    def plane_peer(k):
        return rem(y + div(k, NX), NY) * NX + rem(x + rem(k, NX), NX)

    a = (1 - c) * x + c * y
    b = (1 - c) * y + c * x

    def blk(ao, bo):
        aa, bb = rem(a + ao, 4), rem(b + bo, 4)
        return (1 - c) * (bb * 4 + aa) + c * (aa * 4 + bb)

    def frame_dev(ao, bo):
        return dev(z, blk(ao, bo), c)

    wrow = m8(c * WROWS, WROWS)
    a_next, a_prev = frame_dev(1, 0), frame_dev(3, 0)
    b_next, b_prev = frame_dev(0, 1), frame_dev(0, 3)
    OFF = (0, 3, 1, 2)

    own_kv = kv_v.at[s]
    local(k_h, kv_v.at[s, 0], loc.at[0])
    local(v_h, kv_v.at[s, 1], loc.at[1])
    local(w_h, w_v.at[e], loc.at[2])
    local(q_h, q_v, loc.at[3])
    local(x_h, x_v, loc.at[4])
    gcol = m8(t * HALF_D, HALF_D)
    local(gain_h, gain_v.at[:, pl.ds(gcol, HALF_D)], loc.at[5])
    icol = m8(zh * TOK, TOK)
    local(ids_h, ids_v.at[:, pl.ds(icol, TOK)], loc.at[6])
    local(gat_h, gat_v.at[:, pl.ds(icol, TOK)], loc.at[7])

    barrier = pltpu.get_barrier_semaphore()

    def greet(who):
        pl.semaphore_signal(barrier, inc=1, device_id=who, device_id_type=MESH)

    for who in (other, partner, cross, zh_next, zh_prev, zh_opp):
        greet(who)
    greet(dev(zmod(z - 1 + 2 * t), e, c))

    def greet_plane(k, carry):
        greet(dev(z, plane_peer(k), c))
        return carry

    lax.fori_loop(1, NP, greet_plane, 0)
    wait(kv_v.at[s, 0], loc.at[0])
    wait(kv_v.at[s, 1], loc.at[1])
    wait(w_v.at[e], loc.at[2])
    wait(gain_v.at[:, pl.ds(gcol, HALF_D)], loc.at[5])
    wait(ids_v.at[:, pl.ds(icol, TOK)], loc.at[6])
    wait(gat_v.at[:, pl.ds(icol, TOK)], loc.at[7])
    pl.semaphore_wait(barrier, 7 + NP - 1)

    send(own_kv, own_kv, kv_s.at[0], kv_r.at[0], zh_next)
    send(own_kv, own_kv, kv_s.at[1], kv_r.at[1], zh_prev)
    send(own_kv, own_kv, kvc_s.at[0], kvc_r.at[0], other)
    for n, who in enumerate((zh_next, zh_prev, zh_opp)):
        ids_mine = ids_v.at[:, pl.ds(icol, TOK)]
        gat_mine = gat_v.at[:, pl.ds(icol, TOK)]
        send(ids_mine, ids_mine, sm_s.at[n], sm_r.at[n], who)
        send(gat_mine, gat_mine, sm_s.at[3 + n], sm_r.at[3 + n], who)
    gain_mine = gain_v.at[:, pl.ds(gcol, HALF_D)]
    send(gain_mine, gain_mine, sm_s.at[6], sm_r.at[6], partner)

    def wpart(i, row0, rows):
        return w_v.at[i, pl.ds(m8(wrow + row0, 512), rows), :]

    mine = wpart(blk(0, 0), 0, WROWS)
    send(mine, mine, wa_s, wa_r.at[0], a_next)
    send(mine, mine, wa_s, wa_r.at[1], a_prev)
    send(mine, mine, wb_s, wb_r.at[0, 0], b_next)
    send(mine, mine, wb_s, wb_r.at[0, 1], b_prev)

    def on_chip(i):
        part = wpart(i, 0, WROWS)
        send(part, part, wc_s, wc_r, other)

    def spread_b(n):
        part = wpart(blk(OFF[n], 0), 0, WROWS)
        send(part, part, wb_s, wb_r.at[n, 0], b_next)
        send(part, part, wb_s, wb_r.at[n, 1], b_prev)

    hcol = m8(t * FFH, 128)
    gcolz = m8((1 - t) * FFH, 128)

    @pl.when(giver == 0)
    def _():
        for n, (src, dst) in enumerate(
            (
                (wg_h, wg_v.at[:, pl.ds(hcol, FFH)]),
                (wu_h, wu_v.at[:, pl.ds(hcol, FFH)]),
                (wd_h, wd_v.at[pl.ds(hcol, FFH), :]),
            )
        ):
            local(src, dst, hk.at[n])
            send(src, dst, wk_s.at[n], hk.at[n], other)

    left_kv = kv_v.at[rem(zh + 3, 4) * 2 + c]
    right_kv = kv_v.at[rem(zh + 1, 4) * 2 + c]
    opp = rem(zh + 2, 4) * 2 + c
    wait(own_kv, kv_r.at[0])
    send(left_kv.at[0], left_kv.at[0], kv2_s.at[0], kv2_r.at[0], zh_next)
    send(left_kv, left_kv, kvc_s.at[1], kvc_r.at[1], other)
    wait(own_kv, kv_r.at[1])
    send(right_kv.at[1], right_kv.at[1], kv2_s.at[1], kv2_r.at[1], zh_prev)
    send(right_kv, right_kv, kvc_s.at[2], kvc_r.at[2], other)

    wait(mine, wa_r.at[0])
    part = wpart(blk(3, 0), 0, 512)
    send(part, part, wa_s, wa2_r.at[0], a_next)
    wait(mine, wa_r.at[1])
    part = wpart(blk(1, 0), 512, 512)
    send(part, part, wa_s, wa2_r.at[1], a_prev)
    spread_b(1)
    spread_b(2)
    on_chip(blk(3, 0))
    on_chip(blk(1, 0))

    wait(kv_v.at[opp, 0], kv2_r.at[0])
    wait(kv_v.at[opp, 1], kv2_r.at[1])
    send(kv_v.at[opp], kv_v.at[opp], kvc_s.at[3], kvc_r.at[3], other)

    def wchunks(h):
        col = m8(h * FFH, 128)
        out = []
        for f in range(NF):
            out.append((wg_h.at[pl.ds(f * FC, FC), :], wg_v.at[pl.ds(f * FC, FC), pl.ds(col, FFH)]))
            out.append((wu_h.at[pl.ds(f * FC, FC), :], wu_v.at[pl.ds(f * FC, FC), pl.ds(col, FFH)]))
        for f in ORDER:
            out.append((wd_h.at[:, pl.ds(f * FC, FC)], wd_v.at[pl.ds(col, FFH), pl.ds(f * FC, FC)]))
        return out

    mine_chunks = wchunks(t)
    their_chunks = wchunks(1 - t)

    @pl.when(giver == 1)
    def _():
        for n, (src, dst) in enumerate(mine_chunks):
            send(src, dst, wz_s.at[n], hz.at[n], cross)

    def weights_in(n):
        dst = their_chunks[n][1]
        wait(dst, hz.at[n])

        @pl.when(giver == 1)
        def _():
            send(dst, dst, wf_s.at[n], hz.at[n], other)

    wait(wpart(blk(2, 0), 0, 512), wa2_r.at[0])
    wait(wpart(blk(2, 0), 512, 512), wa2_r.at[1])
    spread_b(3)
    on_chip(blk(2, 0))

    for n in range(3):
        wait(ids_v.at[:, pl.ds(icol, TOK)], sm_r.at[n])
        wait(gat_v.at[:, pl.ds(icol, TOK)], sm_r.at[3 + n])
    ids = ids_v[...]
    gates = gat_v[...]
    mine_ids = NP * z + lax.broadcasted_iota(jnp.int32, (NP, TOKS), 0)
    member = jnp.zeros((NP, TOKS), F32)
    gate_of = jnp.zeros((NP, TOKS), F32)
    for k in range(8):
        hit = ids[k : k + 1, :] == mine_ids
        member = jnp.where(hit, 1.0, member)
        gate_of = jnp.where(hit, gates[k : k + 1, :], gate_of)
    before = (
        lax.broadcasted_iota(jnp.int32, (TOK, TOK), 0) < lax.broadcasted_iota(jnp.int32, (TOK, TOK), 1)
    ).astype(BF)
    places = []
    for n in range(NBLK):
        mb = member[:, n * TOK : (n + 1) * TOK]
        rank = jnp.dot(mb.astype(BF), before, preferred_element_type=F32)
        places.append(jnp.where(mb > 0.5, rank + float(n * CAP), -1.0))
    place = jnp.concatenate(places, axis=1)
    row_id = lax.broadcasted_iota(jnp.int32, (MSG, TOKS), 0).astype(F32)
    for j in range(NP):
        hit = jnp.broadcast_to(place[j : j + 1, :], (MSG, TOKS)) == row_id
        p_v[j * MSG : (j + 1) * MSG, :] = jnp.where(hit, 1.0, 0.0).astype(BF)
        gt_v[j * MSG : (j + 1) * MSG, :] = jnp.where(
            hit, jnp.broadcast_to(gate_of[j : j + 1, :], (MSG, TOKS)), 0.0
        )
    for j in range(ROWS // 128):
        g_v[:, j * 128 : (j + 1) * 128] = gt_v[j * 128 : (j + 1) * 128, :].T.astype(BF)

    for n in range(4):
        wait(own_kv, kvc_r.at[n])
    wait(q_v, loc.at[3])
    softmax_scale = 1.0 / math.sqrt(HEAD)
    allowed = lax.broadcasted_iota(jnp.int32, (2 * TOK, 8 * TOK), 1) <= (
        s * TOK + rem(lax.broadcasted_iota(jnp.int32, (2 * TOK, 8 * TOK), 0), TOK)
    )

    def heads_pair(i, carry):
        g = div(i, 4)
        lane = m8(i * 256, 256)
        kl = m8(g * HEAD, HEAD)
        qq = jnp.concatenate(
            [q_v[:, pl.ds(lane, HEAD)], q_v[:, pl.ds(m8(lane + HEAD, HEAD), HEAD)]], axis=0
        )
        kk = kv_v[:, 0, :, pl.ds(kl, HEAD)].reshape(8 * TOK, HEAD)
        vv = kv_v[:, 1, :, pl.ds(kl, HEAD)].reshape(8 * TOK, HEAD)
        sc = lax.dot_general(qq, kk, (((1,), (1,)), ((), ())), preferred_element_type=F32)
        sc = jnp.where(allowed, sc * softmax_scale, -1e30)
        top = jnp.max(sc, axis=1, keepdims=True)
        p = jnp.exp(sc - top)
        tot = jnp.sum(p, axis=1, keepdims=True)
        o = jnp.dot(p.astype(BF), vv, preferred_element_type=F32) / tot
        o = o.astype(BF)
        attn_v[:, pl.ds(lane, HEAD)] = o[:TOK]
        attn_v[:, pl.ds(m8(lane + HEAD, HEAD), HEAD)] = o[TOK:]
        return carry

    def second_axis(n):
        wait(mine, wb_r.at[n, 0])
        fwd = wpart(blk(OFF[n], 3), 0, 512)
        send(fwd, fwd, wb_s, wb2_r.at[n, 0], b_next)
        on_chip(blk(OFF[n], 3))
        wait(mine, wb_r.at[n, 1])
        fwd = wpart(blk(OFF[n], 1), 512, 512)
        send(fwd, fwd, wb_s, wb2_r.at[n, 1], b_prev)
        on_chip(blk(OFF[n], 1))

    for grp in range(4):
        lax.fori_loop(2 * grp, 2 * grp + 2, heads_pair, 0)
        second_axis(grp)
    for n in range(4):
        wait(wpart(blk(OFF[n], 2), 0, 512), wb2_r.at[n, 0])
        wait(wpart(blk(OFF[n], 2), 512, 512), wb2_r.at[n, 1])
        on_chip(blk(OFF[n], 2))
    wait(w_v.at[pl.ds(0, 15), pl.ds(0, WROWS), :], wc_r)

    my_row = m8(t * HALF_TOK, HALF_TOK)
    their_row = m8((1 - t) * HALF_TOK, HALF_TOK)
    for f in range(NF):

        def project(i, carry):
            wb = f * 4 + i * 2
            ww = jnp.concatenate([w_v[wb], w_v[wb + 1]], axis=1)
            r = jnp.dot(attn_v[...], ww, preferred_element_type=F32)
            ph_v[f, :, pl.ds(m8(i * 256, 256), 256)] = r.astype(BF)
            return carry

        lax.fori_loop(0, 2, project, 0)
        send(ph_v.at[f, pl.ds(their_row, HALF_TOK), :], px_v.at[f], px_s.at[f], px_r.at[f], partner)
    their_f = (1 - t) * 2
    send(
        ph_v.at[pl.ds(their_f, 2), pl.ds(my_row, HALF_TOK), :], px2_v, px2_s, px2_r, partner
    )
    wait(x_v, loc.at[4])
    wait(gain_v.at[:, pl.ds(gcol, HALF_D)], sm_r.at[6])
    power = jnp.zeros((HALF_TOK, 1), F32)
    for f in range(NF):
        wait(px_v.at[f], px_r.at[f])
        mix = (
            x_v[pl.ds(my_row, HALF_TOK), f * FC : (f + 1) * FC].astype(F32)
            + ph_v[f, pl.ds(my_row, HALF_TOK), :].astype(F32)
            + px_v[f].astype(F32)
        )
        mix_v[f] = mix
        power = power + jnp.sum(mix * mix, axis=1, keepdims=True)
    inverse = lax.rsqrt(power / D + 1e-06)

    zrow = m8(z * HALF_TOK, HALF_TOK)
    for f in range(NF):
        gain = gain_v[:, f * FC : (f + 1) * FC]
        xg_v[f, pl.ds(zrow, HALF_TOK), :] = (mix_v[f] * inverse * gain).astype(BF)
        shard = xg_v.at[f, pl.ds(zrow, HALF_TOK), :]
        send(shard, shard, xg_s.at[0], xg_r.at[f, 0, 0], z_next)
        send(shard, shard, xg_s.at[1], xg_r.at[f, 1, 0], z_prev)

    def reach(f, d):
        return 4 if (f + d) % 2 == 0 else 3

    def ring_step(f, k):
        for d in range(2):
            if k > reach(f, d):
                continue
            src_z = zmod(z - k) if d == 0 else zmod(z + k)
            shard = xg_v.at[f, pl.ds(m8(src_z * HALF_TOK, HALF_TOK), HALF_TOK), :]
            wait(shard, xg_r.at[f, d, k - 1])
            if k + 1 <= reach(f, d):
                send(shard, shard, xg_s.at[d], xg_r.at[f, d, k], z_next if d == 0 else z_prev)

    my_slot = pl.ds(m8(e * MSG, 16), MSG)

    def exchange(buf, dst, f, ss, rs, ls):
        def one(k, carry):
            peer = plane_peer(k)
            send(
                buf.at[f, pl.ds(m8(peer * MSG, 16), MSG), :],
                dst.at[f, my_slot, :],
                ss.at[f],
                rs.at[f],
                dev(z, peer, c),
            )
            return carry

        lax.fori_loop(1, NP, one, 0)
        local(buf.at[f, my_slot, :], dst.at[f, my_slot, :], ls.at[f])

    FIFTEEN = (NP - 1) * MSG

    def exchanged(dst, f, rs, ls):
        wait(dst.at[f, pl.ds(0, FIFTEEN), :], rs.at[f])
        wait(dst.at[f, my_slot, :], ls.at[f])

    def pick_rows(f):
        def group(i, carry):
            rows = pl.ds(m8(i * 256, 256), 256)
            s_v[f, rows, :] = jnp.dot(p_v[rows, :], xg_v[f], preferred_element_type=F32).astype(BF)
            return carry

        lax.fori_loop(0, ROWS // 256, group, 0)
        exchange(s_v, r_v, f, dsp_s, dsp_r, dsp_l)

    for wave in range(1, NF + 4):
        for f in range(NF):
            k = wave - f
            if 1 <= k <= 4:
                ring_step(f, k)
                if k == 4:
                    pick_rows(f)

    wait(px2_v, px2_r)
    my_f = t * 2
    for u in range(2):
        cols = pl.ds(m8(gcol + u * FC, FC), FC)
        mixo_v[u, pl.ds(my_row, HALF_TOK), :] = mix_v[my_f + u]
        mixo_v[u, pl.ds(their_row, HALF_TOK), :] = (
            x_v[pl.ds(their_row, HALF_TOK), cols].astype(F32)
            + ph_v[my_f + u, pl.ds(their_row, HALF_TOK), :].astype(F32)
            + px2_v[u].astype(F32)
        )

    wait(wg_v.at[:, pl.ds(hcol, FFH)], hk.at[0])
    wait(wu_v.at[:, pl.ds(hcol, FFH)], hk.at[1])
    for f in range(NF):
        weights_in(2 * f)
        weights_in(2 * f + 1)
        exchanged(r_v, f, dsp_r, dsp_l)

        def gate_up(i, carry):
            rows = pl.ds(m8(i * 256, 256), 256)
            rr = r_v[f, rows, :]
            ga = jnp.dot(rr, wg_v[f * FC : (f + 1) * FC, :], preferred_element_type=F32)
            ua = jnp.dot(rr, wu_v[f * FC : (f + 1) * FC, :], preferred_element_type=F32)
            if f > 0:
                ga = ga + ag_v[rows, :]
                ua = ua + au_v[rows, :]
            if f < NF - 1:
                ag_v[rows, :] = ga
                au_v[rows, :] = ua
            else:
                hid_v[rows, :] = (ga / (1.0 + jnp.exp(-ga)) * ua).astype(BF)
            return carry

        lax.fori_loop(0, ROWS // 256, gate_up, 0)

    wait(wd_v.at[pl.ds(hcol, FFH), :], hk.at[2])
    for n, f in enumerate(ORDER):
        weights_in(8 + n)

        def down(i, carry):
            rows = pl.ds(m8(i * 256, 256), 256)
            cols = slice(f * FC, (f + 1) * FC)
            y0 = jnp.dot(hid_v[rows, :FFH], wd_v[:FFH, cols], preferred_element_type=F32)
            y1 = jnp.dot(hid_v[rows, FFH:], wd_v[FFH:, cols], preferred_element_type=F32)
            y_v[f, rows, :] = (y0.astype(BF).astype(F32) + y1.astype(BF).astype(F32)).astype(BF)
            return carry

        lax.fori_loop(0, ROWS // 256, down, 0)
        exchange(y_v, yr_v, f, ret_s, ret_r, ret_l)

    def combine(f):
        exchanged(yr_v, f, ret_r, ret_l)

        def group(i, carry):
            rows = pl.ds(m8(i * 256, 256), 256)
            o_v[f, rows, :] = jnp.dot(g_v[rows, :], yr_v[f], preferred_element_type=F32)
            return carry

        lax.fori_loop(0, TOKS // 256, group, 0)

    def own_part(dest, u):
        return o_v[rem(dest, 2) * 2 + u, pl.ds(m8(div(dest, 2) * TOK, TOK), TOK), :]

    def far(u, d):
        return 4 if (u + d) % 2 == 0 else 3

    def sum_step(u, i):
        for d in range(2):
            dist = far(u, d) - i
            if dist < 1:
                continue
            dest = zmod(z + dist) if d == 0 else zmod(z - dist)
            part = own_part(dest, u)
            if i > 0:
                slot = rs_r.at[u, d, dist]
                wait(slot, rs_rs.at[u, d, dist])
                part = part + rs_r[u, d, dist].astype(F32)
            rs_s[u, d, dist - 1] = part.astype(BF)
            send(
                rs_s.at[u, d, dist - 1],
                rs_r.at[u, d, dist - 1],
                rs_ss.at[u, d, dist - 1],
                rs_rs.at[u, d, dist - 1],
                z_next if d == 0 else z_prev,
            )

    def finish(u):
        for d in range(2):
            wait(rs_r.at[u, d, 0], rs_rs.at[u, d, 0])
        out_ref[:, u * FC : (u + 1) * FC] = (
            mixo_v[u]
            + (own_part(z, u) + rs_r[u, 0, 0].astype(F32) + rs_r[u, 1, 0].astype(F32))
        ).astype(BF)

    combine(0)
    combine(2)
    sum_step(0, 0)
    combine(1)
    sum_step(0, 1)
    combine(3)
    sum_step(1, 0)
    sum_step(0, 2)
    sum_step(1, 1)
    sum_step(0, 3)
    sum_step(1, 2)
    finish(0)
    sum_step(1, 3)
    finish(1)

    for n in range(2):
        wait(own_kv, kv_s.at[n])
        wait(own_kv.at[0], kv2_s.at[n])
    for n in range(4):
        wait(own_kv, kvc_s.at[n])
    for n in range(3):
        wait(ids_v.at[:, pl.ds(0, TOK)], sm_s.at[n])
        wait(gat_v.at[:, pl.ds(0, TOK)], sm_s.at[3 + n])
    wait(gain_mine, sm_s.at[6])
    wait(w_v.at[pl.ds(0, 3), pl.ds(0, WROWS), :], wa_s)
    wait(w_v.at[pl.ds(0, 12), pl.ds(0, WROWS), :], wb_s)
    wait(w_v.at[pl.ds(0, 15), pl.ds(0, WROWS), :], wc_s)
    for f in range(NF):
        wait(px_v.at[f], px_s.at[f])
        wait(s_v.at[f, pl.ds(0, FIFTEEN), :], dsp_s.at[f])
        wait(y_v.at[f, pl.ds(0, FIFTEEN), :], ret_s.at[f])
    wait(px2_v, px2_s)
    for d in range(2):
        wait(xg_v.at[pl.ds(0, 2), pl.ds(0, 7 * HALF_TOK), :], xg_s.at[d])
        for u in range(2):
            for n in range(far(u, d)):
                wait(rs_s.at[u, d, n], rs_ss.at[u, d, n])

    @pl.when(giver == 0)
    def _():
        wait(wg_h, wk_s.at[0])
        wait(wu_h, wk_s.at[1])
        wait(wd_h, wk_s.at[2])

    @pl.when(giver == 1)
    def _():
        for n in range(12):
            wait(mine_chunks[n][1], wz_s.at[n])
            wait(mine_chunks[n][1], wf_s.at[n])


def per_device(
    q_rows, k_rows, value_rows, x_rows, out_weight, norm_gain, w_gate, w_up, w_down, expert_ids, gate_weights
):
    dma = pltpu.SemaphoreType.DMA
    any_spec = pl.BlockSpec(memory_space=pl.ANY)
    out = pl.pallas_call(
        layer_kernel,
        out_shape=jax.ShapeDtypeStruct((TOK, HALF_D), BF),
        in_specs=[any_spec] * 11,
        out_specs=pl.BlockSpec(memory_space=pltpu.VMEM),
        scratch_shapes=[
            pltpu.VMEM((TOK, D), BF),
            pltpu.VMEM((TOK, D), BF),
            pltpu.VMEM((8, 2, TOK, 256), BF),
            pltpu.VMEM((NP, D, 128), BF),
            pltpu.VMEM((1, D), F32),
            pltpu.VMEM((8, TOKS), jnp.int32),
            pltpu.VMEM((8, TOKS), F32),
            pltpu.VMEM((TOK, D), BF),
            pltpu.VMEM((NF, TOK, FC), BF),
            pltpu.VMEM((NF, HALF_TOK, FC), BF),
            pltpu.VMEM((2, HALF_TOK, FC), BF),
            pltpu.VMEM((NF, HALF_TOK, FC), F32),
            pltpu.VMEM((2, TOK, FC), F32),
            pltpu.VMEM((NF, TOKS, FC), BF),
            pltpu.VMEM((ROWS, TOKS), BF),
            pltpu.VMEM((ROWS, TOKS), F32),
            pltpu.VMEM((TOKS, ROWS), BF),
            pltpu.VMEM((NF, ROWS, FC), BF),
            pltpu.VMEM((NF, ROWS, FC), BF),
            pltpu.VMEM((D, FF), BF),
            pltpu.VMEM((D, FF), BF),
            pltpu.VMEM((FF, D), BF),
            pltpu.VMEM((ROWS, FF), F32),
            pltpu.VMEM((ROWS, FF), F32),
            pltpu.VMEM((ROWS, FF), BF),
            pltpu.VMEM((NF, ROWS, FC), BF),
            pltpu.VMEM((NF, ROWS, FC), BF),
            pltpu.VMEM((NF, TOKS, FC), F32),
            pltpu.VMEM((2, 2, 4, TOK, FC), BF),
            pltpu.VMEM((2, 2, 4, TOK, FC), BF),
            dma((8,)), dma((3,)), dma((12,)), dma((12,)), dma((3,)), dma((12,)),
            dma((2,)), dma((2,)), dma((4,)), dma((4,)), dma((2,)), dma((2,)),
            dma((7,)), dma((7,)),
            dma, dma((2,)), dma((2,)), dma, dma((4, 2)), dma((4, 2)), dma, dma,
            dma((NF,)), dma((NF,)), dma, dma,
            dma((2,)), dma((NF, 2, 4)), dma((NF,)), dma((NF,)), dma((NF,)), dma((NF,)), dma((NF,)), dma((NF,)),
            dma((2, 2, 4)), dma((2, 2, 4)),
        ],
        compiler_params=pltpu.CompilerParams(
            collective_id=0, has_side_effects=True, vmem_limit_bytes=62 * 1024 * 1024
        ),
        name="layer",
    )(
        q_rows[0],
        k_rows[0],
        value_rows[0],
        x_rows[0],
        out_weight,
        norm_gain.reshape(1, HALF_D),
        w_gate[0],
        w_up[0],
        w_down[0],
        expert_ids[0].T,
        gate_weights[0].T,
    )
    return out[None]


def solution(mesh):
    return jax.shard_map(
        per_device,
        mesh=mesh,
        in_specs=(
            P("expert", "seq", "tensor"),
            P("expert", "seq", "tensor"),
            P("expert", "seq", "tensor"),
            P("expert", "seq", None),
            P("tensor", "expert"),
            P("tensor"),
            P(("seq", "expert"), None, "tensor"),
            P(("seq", "expert"), None, "tensor"),
            P(("seq", "expert"), "tensor", None),
            P("expert", "seq", None),
            P("expert", "seq", None),
        ),
        out_specs=P("expert", "seq", "tensor"),
        check_vma=False,
    )
```

```python
import math

import jax
import jax.numpy as jnp
from jax import lax
from jax.experimental import pallas as pl
from jax.experimental.pallas import tpu as pltpu
from jax.sharding import PartitionSpec as P

MESH = pl.DeviceIdType.MESH
BF = jnp.bfloat16
F32 = jnp.float32

NX, NY, NZ = 4, 4, 8
NP = NX * NY
HEAD = 128
TOK = 128
HALF_TOK = 64
D = 2048
CAP = 12
NBLK = 4
MSG = NBLK * CAP
ROWS = NP * MSG
TOKS = NBLK * TOK
NF = 4
FC = D // NF
FFH = 384
FF = 768
HALF_D = D // 2
WROWS = 1024
NR = 8
RC = D // NR
NU = NR // 2
PAIRS = tuple(h * NU + u for u in range(NU) for h in range(2))


def layer_kernel(
    q_h, k_h, v_h, x_h, w_h, gain_h, wg_h, wu_h, wd_h, ids_h, gat_h,
    out_ref,
    q_v, x_v, kv_v, w_v, gain_v, ids_v, gat_v,
    attn_v, ph_v, px_v, px2_v, mix_v, mixo_v,
    xg_v, p_v, gt_v, g_v, s_v, r_v,
    wg_v, wu_v, wd_v, ag_v, au_v, hid_v,
    y_v, yr_v, o_v, rs_s, rs_r,
    loc, hk, hz, wz_s, wk_s, wf_s,
    kv_s, kv_r, kvc_s, kvc_r, kv2_s, kv2_r,
    sm_s, sm_r,
    wa_s, wa_r, wa2_r, wb_s, wb_r, wb2_r, wc_s, wc_r,
    px_s, px_r, px2_s, px2_r,
    xg_s, xg_r, dsp_s, dsp_r, dsp_l, ret_s, ret_r, ret_l,
    rs_ss, rs_rs,
):
    rem, div = lax.rem, lax.div
    s = lax.axis_index("seq")
    e = lax.axis_index("expert")
    t = lax.axis_index("tensor")
    zh = div(s, 2)
    c = rem(s, 2)
    z = zh * 2 + t
    y = div(e, NX)
    x = rem(e, NX)
    oc = 1 - c
    giver = rem(c + t, 2)

    def dev(zz, ee, cc):
        return (div(zz, 2) * 2 + cc, ee, rem(zz, 2))

    def zmod(v):
        return rem(v + NZ, NZ)

    def send(src, dst, ss, rs, who):
        cp = pltpu.make_async_remote_copy(
            src_ref=src, dst_ref=dst, send_sem=ss, recv_sem=rs, device_id=who, device_id_type=MESH
        )
        cp.start()

    def local(src, dst, sem):
        pltpu.make_async_copy(src, dst, sem).start()

    def wait(ref, sem):
        pltpu.make_async_copy(ref, ref, sem).wait()

    def m8(v, n):
        return pl.multiple_of(v, n)

    other = dev(z, e, oc)
    partner = dev(z + 1 - 2 * t, e, c)
    cross = dev(z + 1 - 2 * t, e, oc)
    z_next, z_prev = dev(zmod(z + 1), e, c), dev(zmod(z - 1), e, c)
    zh_next, zh_prev = dev(zmod(z + 2), e, c), dev(zmod(z - 2), e, c)
    zh_opp = dev(zmod(z + 4), e, c)

    def plane_peer(k):
        return rem(y + div(k, NX), NY) * NX + rem(x + rem(k, NX), NX)

    a = (1 - c) * x + c * y
    b = (1 - c) * y + c * x

    def blk(ao, bo):
        aa, bb = rem(a + ao, 4), rem(b + bo, 4)
        return (1 - c) * (bb * 4 + aa) + c * (aa * 4 + bb)

    def frame_dev(ao, bo):
        return dev(z, blk(ao, bo), c)

    wrow = m8(c * WROWS, WROWS)
    a_next, a_prev = frame_dev(1, 0), frame_dev(3, 0)
    b_next, b_prev = frame_dev(0, 1), frame_dev(0, 3)
    OFF = (0, 3, 1, 2)

    own_kv = kv_v.at[s]
    local(k_h, kv_v.at[s, 0], loc.at[0])
    local(v_h, kv_v.at[s, 1], loc.at[1])
    local(w_h, w_v.at[e], loc.at[2])
    local(q_h, q_v, loc.at[3])
    local(x_h, x_v, loc.at[4])
    gcol = m8(t * HALF_D, HALF_D)
    local(gain_h, gain_v.at[:, pl.ds(gcol, HALF_D)], loc.at[5])
    icol = m8(zh * TOK, TOK)
    local(ids_h, ids_v.at[:, pl.ds(icol, TOK)], loc.at[6])
    local(gat_h, gat_v.at[:, pl.ds(icol, TOK)], loc.at[7])

    barrier = pltpu.get_barrier_semaphore()

    def greet(who):
        pl.semaphore_signal(barrier, inc=1, device_id=who, device_id_type=MESH)

    for who in (other, partner, cross, zh_next, zh_prev, zh_opp):
        greet(who)
    greet(dev(zmod(z - 1 + 2 * t), e, c))

    def greet_plane(k, carry):
        greet(dev(z, plane_peer(k), c))
        return carry

    lax.fori_loop(1, NP, greet_plane, 0)
    wait(kv_v.at[s, 0], loc.at[0])
    wait(kv_v.at[s, 1], loc.at[1])
    wait(w_v.at[e], loc.at[2])
    wait(gain_v.at[:, pl.ds(gcol, HALF_D)], loc.at[5])
    wait(ids_v.at[:, pl.ds(icol, TOK)], loc.at[6])
    wait(gat_v.at[:, pl.ds(icol, TOK)], loc.at[7])
    pl.semaphore_wait(barrier, 7 + NP - 1)

    def kv_part(i, n):
        return kv_v.at[i, n]

    for n in range(2):
        send(kv_part(s, n), kv_part(s, n), kv_s.at[0, n], kv_r.at[0, n], zh_next)
        send(kv_part(s, 1 - n), kv_part(s, 1 - n), kv_s.at[1, 1 - n], kv_r.at[1, 1 - n], zh_prev)
    send(own_kv, own_kv, kvc_s.at[0], kvc_r.at[0], other)
    for n, who in enumerate((zh_next, zh_prev, zh_opp)):
        ids_mine = ids_v.at[:, pl.ds(icol, TOK)]
        gat_mine = gat_v.at[:, pl.ds(icol, TOK)]
        send(ids_mine, ids_mine, sm_s.at[n], sm_r.at[n], who)
        send(gat_mine, gat_mine, sm_s.at[3 + n], sm_r.at[3 + n], who)
    gain_mine = gain_v.at[:, pl.ds(gcol, HALF_D)]
    send(gain_mine, gain_mine, sm_s.at[6], sm_r.at[6], partner)

    def wpart(i, row0, rows):
        return w_v.at[i, pl.ds(m8(wrow + row0, 512), rows), :]

    mine = wpart(blk(0, 0), 0, WROWS)
    send(mine, mine, wa_s, wa_r.at[0], a_next)
    send(mine, mine, wa_s, wa_r.at[1], a_prev)
    send(mine, mine, wb_s, wb_r.at[0, 0], b_next)
    send(mine, mine, wb_s, wb_r.at[0, 1], b_prev)

    def on_chip(i):
        part = wpart(i, 0, WROWS)
        send(part, part, wc_s, wc_r, other)

    def spread_b(n):
        part = wpart(blk(OFF[n], 0), 0, WROWS)
        send(part, part, wb_s, wb_r.at[n, 0], b_next)
        send(part, part, wb_s, wb_r.at[n, 1], b_prev)

    hcol = m8(t * FFH, 128)
    gcolz = m8((1 - t) * FFH, 128)

    @pl.when(giver == 0)
    def _():
        for n, (src, dst) in enumerate(
            (
                (wg_h, wg_v.at[:, pl.ds(hcol, FFH)]),
                (wu_h, wu_v.at[:, pl.ds(hcol, FFH)]),
                (wd_h, wd_v.at[pl.ds(hcol, FFH), :]),
            )
        ):
            local(src, dst, hk.at[n])
            send(src, dst, wk_s.at[n], hk.at[n], other)

    left = rem(zh + 3, 4) * 2 + c
    right = rem(zh + 1, 4) * 2 + c
    opp = rem(zh + 2, 4) * 2 + c
    wait(kv_part(left, 0), kv_r.at[0, 0])
    send(kv_part(left, 0), kv_part(left, 0), kv2_s.at[0], kv2_r.at[0], zh_next)
    wait(kv_part(right, 1), kv_r.at[1, 1])
    send(kv_part(right, 1), kv_part(right, 1), kv2_s.at[1], kv2_r.at[1], zh_prev)

    wait(mine, wa_r.at[0])
    part = wpart(blk(3, 0), 0, 512)
    send(part, part, wa_s, wa2_r.at[0], a_next)
    wait(mine, wa_r.at[1])
    part = wpart(blk(1, 0), 512, 512)
    send(part, part, wa_s, wa2_r.at[1], a_prev)
    spread_b(1)
    spread_b(2)
    on_chip(blk(3, 0))
    on_chip(blk(1, 0))

    wait(kv_part(left, 1), kv_r.at[0, 1])
    send(kv_v.at[left], kv_v.at[left], kvc_s.at[1], kvc_r.at[1], other)
    wait(kv_part(right, 0), kv_r.at[1, 0])
    send(kv_v.at[right], kv_v.at[right], kvc_s.at[2], kvc_r.at[2], other)

    def wchunks(h):
        col = m8(h * FFH, 128)
        out = []
        for f in range(NF):
            out.append((wg_h.at[pl.ds(f * FC, FC), :], wg_v.at[pl.ds(f * FC, FC), pl.ds(col, FFH)]))
            out.append((wu_h.at[pl.ds(f * FC, FC), :], wu_v.at[pl.ds(f * FC, FC), pl.ds(col, FFH)]))
        for f in PAIRS:
            out.append((wd_h.at[:, pl.ds(f * RC, RC)], wd_v.at[pl.ds(col, FFH), pl.ds(f * RC, RC)]))
        return out

    mine_chunks = wchunks(t)
    their_chunks = wchunks(1 - t)

    def swap(lo, hi):
        @pl.when(giver == 1)
        def _():
            for n in range(lo, hi):
                src, dst = mine_chunks[n]
                send(src, dst, wz_s.at[n], hz.at[n], cross)

    def weights_in(n):
        dst = their_chunks[n][1]
        wait(dst, hz.at[n])

        @pl.when(giver == 1)
        def _():
            send(dst, dst, wf_s.at[n], hz.at[n], other)

    wait(wpart(blk(2, 0), 0, 512), wa2_r.at[0])
    wait(wpart(blk(2, 0), 512, 512), wa2_r.at[1])
    spread_b(3)
    on_chip(blk(2, 0))

    def second_axis(n):
        wait(mine, wb_r.at[n, 0])
        fwd = wpart(blk(OFF[n], 3), 0, 512)
        send(fwd, fwd, wb_s, wb2_r.at[n, 0], b_next)
        on_chip(blk(OFF[n], 3))
        wait(mine, wb_r.at[n, 1])
        fwd = wpart(blk(OFF[n], 1), 512, 512)
        send(fwd, fwd, wb_s, wb2_r.at[n, 1], b_prev)
        on_chip(blk(OFF[n], 1))

    def second_axis_end(n):
        wait(wpart(blk(OFF[n], 2), 0, 512), wb2_r.at[n, 0])
        wait(wpart(blk(OFF[n], 2), 512, 512), wb2_r.at[n, 1])
        on_chip(blk(OFF[n], 2))

    second_axis(0)

    wait(kv_part(opp, 0), kv2_r.at[0])
    wait(kv_part(opp, 1), kv2_r.at[1])
    send(kv_v.at[opp], kv_v.at[opp], kvc_s.at[3], kvc_r.at[3], other)
    swap(0, 4)

    for n in range(3):
        wait(ids_v.at[:, pl.ds(icol, TOK)], sm_r.at[n])
        wait(gat_v.at[:, pl.ds(icol, TOK)], sm_r.at[3 + n])
    ids = ids_v[...]
    gates = gat_v[...]
    mine_ids = NP * z + lax.broadcasted_iota(jnp.int32, (NP, TOKS), 0)
    member = jnp.zeros((NP, TOKS), F32)
    gate_of = jnp.zeros((NP, TOKS), F32)
    for k in range(8):
        hit = ids[k : k + 1, :] == mine_ids
        member = jnp.where(hit, 1.0, member)
        gate_of = jnp.where(hit, gates[k : k + 1, :], gate_of)
    before = (
        lax.broadcasted_iota(jnp.int32, (TOK, TOK), 0) < lax.broadcasted_iota(jnp.int32, (TOK, TOK), 1)
    ).astype(BF)
    places = []
    for n in range(NBLK):
        mb = member[:, n * TOK : (n + 1) * TOK]
        rank = jnp.dot(mb.astype(BF), before, preferred_element_type=F32)
        places.append(jnp.where(mb > 0.5, rank + float(n * CAP), -1.0))
    place = jnp.concatenate(places, axis=1)
    row_id = lax.broadcasted_iota(jnp.int32, (MSG, TOKS), 0).astype(F32)
    for j in range(NP):
        hit = jnp.broadcast_to(place[j : j + 1, :], (MSG, TOKS)) == row_id
        p_v[j * MSG : (j + 1) * MSG, :] = jnp.where(hit, 1.0, 0.0).astype(BF)
        gt_v[j * MSG : (j + 1) * MSG, :] = jnp.where(
            hit, jnp.broadcast_to(gate_of[j : j + 1, :], (MSG, TOKS)), 0.0
        )
    for j in range(ROWS // 128):
        g_v[:, j * 128 : (j + 1) * 128] = gt_v[j * 128 : (j + 1) * 128, :].T.astype(BF)

    second_axis(1)
    for n in range(4):
        wait(own_kv, kvc_r.at[n])
    wait(q_v, loc.at[3])
    softmax_scale = 1.0 / math.sqrt(HEAD)
    allowed = lax.broadcasted_iota(jnp.int32, (2 * TOK, 8 * TOK), 1) <= (
        s * TOK + rem(lax.broadcasted_iota(jnp.int32, (2 * TOK, 8 * TOK), 0), TOK)
    )

    def heads_pair(i, carry):
        g = div(i, 4)
        lane = m8(i * 256, 256)
        kl = m8(g * HEAD, HEAD)
        qq = jnp.concatenate(
            [q_v[:, pl.ds(lane, HEAD)], q_v[:, pl.ds(m8(lane + HEAD, HEAD), HEAD)]], axis=0
        )
        kk = kv_v[:, 0, :, pl.ds(kl, HEAD)].reshape(8 * TOK, HEAD)
        vv = kv_v[:, 1, :, pl.ds(kl, HEAD)].reshape(8 * TOK, HEAD)
        sc = lax.dot_general(qq, kk, (((1,), (1,)), ((), ())), preferred_element_type=F32)
        sc = jnp.where(allowed, sc * softmax_scale, -1e30)
        top = jnp.max(sc, axis=1, keepdims=True)
        p = jnp.exp(sc - top)
        tot = jnp.sum(p, axis=1, keepdims=True)
        o = jnp.dot(p.astype(BF), vv, preferred_element_type=F32) / tot
        o = o.astype(BF)
        attn_v[:, pl.ds(lane, HEAD)] = o[:TOK]
        attn_v[:, pl.ds(m8(lane + HEAD, HEAD), HEAD)] = o[TOK:]
        return carry

    for grp in range(4):
        lax.fori_loop(2 * grp, 2 * grp + 2, heads_pair, 0)
        if grp == 0:
            second_axis(2)
        if grp == 1:
            second_axis_end(0)
            second_axis(3)
        if grp == 2:
            second_axis_end(1)
    second_axis_end(2)
    second_axis_end(3)
    wait(w_v.at[pl.ds(0, 15), pl.ds(0, WROWS), :], wc_r)

    my_row = m8(t * HALF_TOK, HALF_TOK)
    their_row = m8((1 - t) * HALF_TOK, HALF_TOK)
    for f in range(NF):

        def project(i, carry):
            wb = f * 4 + i * 2
            ww = jnp.concatenate([w_v[wb], w_v[wb + 1]], axis=1)
            r = jnp.dot(attn_v[...], ww, preferred_element_type=F32)
            ph_v[f, :, pl.ds(m8(i * 256, 256), 256)] = r.astype(BF)
            return carry

        lax.fori_loop(0, 2, project, 0)
        send(ph_v.at[f, pl.ds(their_row, HALF_TOK), :], px_v.at[f], px_s.at[f], px_r.at[f], partner)
    wait(x_v, loc.at[4])
    wait(gain_v.at[:, pl.ds(gcol, HALF_D)], sm_r.at[6])
    power = jnp.zeros((HALF_TOK, 1), F32)
    for f in range(NF):
        wait(px_v.at[f], px_r.at[f])
        mix = (
            x_v[pl.ds(my_row, HALF_TOK), f * FC : (f + 1) * FC].astype(F32)
            + ph_v[f, pl.ds(my_row, HALF_TOK), :].astype(F32)
            + px_v[f].astype(F32)
        )
        mix_v[f] = mix
        power = power + jnp.sum(mix * mix, axis=1, keepdims=True)
    inverse = lax.rsqrt(power / D + 1e-06)

    zrow = m8(z * HALF_TOK, HALF_TOK)
    def ring_open(f):
        gain = gain_v[:, f * FC : (f + 1) * FC]
        xg_v[f, pl.ds(zrow, HALF_TOK), :] = (mix_v[f] * inverse * gain).astype(BF)
        shard = xg_v.at[f, pl.ds(zrow, HALF_TOK), :]
        send(shard, shard, xg_s.at[0], xg_r.at[f, 0, 0], z_next)
        send(shard, shard, xg_s.at[1], xg_r.at[f, 1, 0], z_prev)

    def reach(f, d):
        return 4 if (f + d) % 2 == 0 else 3

    def ring_step(f, k):
        for d in range(2):
            if k > reach(f, d):
                continue
            src_z = zmod(z - k) if d == 0 else zmod(z + k)
            shard = xg_v.at[f, pl.ds(m8(src_z * HALF_TOK, HALF_TOK), HALF_TOK), :]
            wait(shard, xg_r.at[f, d, k - 1])
            if k + 1 <= reach(f, d):
                send(shard, shard, xg_s.at[d], xg_r.at[f, d, k], z_next if d == 0 else z_prev)

    my_slot = pl.ds(m8(e * MSG, 16), MSG)

    def exchange(buf, dst, f, ss, rs, ls):
        def one(k, carry):
            peer = plane_peer(k)
            send(
                buf.at[f, pl.ds(m8(peer * MSG, 16), MSG), :],
                dst.at[f, my_slot, :],
                ss.at[f],
                rs.at[f],
                dev(z, peer, c),
            )
            return carry

        lax.fori_loop(1, NP, one, 0)
        local(buf.at[f, my_slot, :], dst.at[f, my_slot, :], ls.at[f])

    FIFTEEN = (NP - 1) * MSG

    def exchanged(dst, f, rs, ls):
        wait(dst.at[f, pl.ds(0, FIFTEEN), :], rs.at[f])
        wait(dst.at[f, my_slot, :], ls.at[f])

    def pick_rows(f):
        def group(i, carry):
            rows = pl.ds(m8(i * 256, 256), 256)
            s_v[f, rows, :] = jnp.dot(p_v[rows, :], xg_v[f], preferred_element_type=F32).astype(BF)
            return carry

        lax.fori_loop(0, ROWS // 256, group, 0)
        exchange(s_v, r_v, f, dsp_s, dsp_r, dsp_l)

    ring_open(0)
    ring_open(1)
    for wave in range(1, NF + 4):
        for f in range(NF):
            if 1 <= wave - f <= 4:
                ring_step(f, wave - f)
        if wave + 1 < NF:
            ring_open(wave + 1)
        if wave == NF + 3:
            their_f = (1 - t) * 2
            mid = ph_v.at[pl.ds(their_f, 2), pl.ds(my_row, HALF_TOK), :]
            send(mid, px2_v, px2_s, px2_r, partner)
            swap(4, 8 + NR)
        if wave >= 4:
            pick_rows(wave - 4)

    wait(px2_v, px2_r)
    my_f = t * 2
    for u in range(2):
        cols = pl.ds(m8(gcol + u * FC, FC), FC)
        mixo_v[u, pl.ds(my_row, HALF_TOK), :] = mix_v[my_f + u]
        mixo_v[u, pl.ds(their_row, HALF_TOK), :] = (
            x_v[pl.ds(their_row, HALF_TOK), cols].astype(F32)
            + ph_v[my_f + u, pl.ds(their_row, HALF_TOK), :].astype(F32)
            + px2_v[u].astype(F32)
        )

    wait(wg_v.at[:, pl.ds(hcol, FFH)], hk.at[0])
    wait(wu_v.at[:, pl.ds(hcol, FFH)], hk.at[1])
    for f in range(NF):
        weights_in(2 * f)
        weights_in(2 * f + 1)
        exchanged(r_v, f, dsp_r, dsp_l)

        def gate_up(i, carry):
            rows = pl.ds(m8(i * 256, 256), 256)
            rr = r_v[f, rows, :]
            ga = jnp.dot(rr, wg_v[f * FC : (f + 1) * FC, :], preferred_element_type=F32)
            ua = jnp.dot(rr, wu_v[f * FC : (f + 1) * FC, :], preferred_element_type=F32)
            if f > 0:
                ga = ga + ag_v[rows, :]
                ua = ua + au_v[rows, :]
            if f < NF - 1:
                ag_v[rows, :] = ga
                au_v[rows, :] = ua
            else:
                hid_v[rows, :] = (ga / (1.0 + jnp.exp(-ga)) * ua).astype(BF)
            return carry

        lax.fori_loop(0, ROWS // 256, gate_up, 0)

    wait(wd_v.at[pl.ds(hcol, FFH), :], hk.at[2])
    for n, f in enumerate(PAIRS):
        weights_in(8 + n)

        def down(i, carry):
            rows = pl.ds(m8(i * 256, 256), 256)
            cols = slice(f * RC, (f + 1) * RC)
            y0 = jnp.dot(hid_v[rows, :FFH], wd_v[:FFH, cols], preferred_element_type=F32)
            y1 = jnp.dot(hid_v[rows, FFH:], wd_v[FFH:, cols], preferred_element_type=F32)
            y_v[f, rows, :] = (y0.astype(BF).astype(F32) + y1.astype(BF).astype(F32)).astype(BF)
            return carry

        lax.fori_loop(0, ROWS // 256, down, 0)
        exchange(y_v, yr_v, f, ret_s, ret_r, ret_l)

    def combine(f):
        exchanged(yr_v, f, ret_r, ret_l)

        def group(i, carry):
            rows = pl.ds(m8(i * 256, 256), 256)
            o_v[f, rows, :] = jnp.dot(g_v[rows, :], yr_v[f], preferred_element_type=F32)
            return carry

        lax.fori_loop(0, TOKS // 256, group, 0)

    def own_part(dest, u):
        return o_v[rem(dest, 2) * NU + u, pl.ds(m8(div(dest, 2) * TOK, TOK), TOK), :]

    def far(u, d):
        return 4 if (u + d) % 2 == 0 else 3

    def sum_step(u, i):
        for d in range(2):
            dist = far(u, d) - i
            if dist < 1:
                continue
            dest = zmod(z + dist) if d == 0 else zmod(z - dist)
            part = own_part(dest, u)
            if i > 0:
                slot = rs_r.at[u, d, dist]
                wait(slot, rs_rs.at[u, d, dist])
                part = part + rs_r[u, d, dist].astype(F32)
            rs_s[u, d, dist - 1] = part.astype(BF)
            send(
                rs_s.at[u, d, dist - 1],
                rs_r.at[u, d, dist - 1],
                rs_ss.at[u, d, dist - 1],
                rs_rs.at[u, d, dist - 1],
                z_next if d == 0 else z_prev,
            )

    def finish(u):
        for d in range(2):
            wait(rs_r.at[u, d, 0], rs_rs.at[u, d, 0])
        lo = (u % 2) * RC
        out_ref[:, u * RC : (u + 1) * RC] = (
            mixo_v[u // 2, :, lo : lo + RC]
            + (own_part(z, u) + rs_r[u, 0, 0].astype(F32) + rs_r[u, 1, 0].astype(F32))
        ).astype(BF)

    for u in range(NU):
        combine(u)
        if u > 0:
            sum_step(u - 1, 2)
        combine(NU + u)
        if u > 0:
            sum_step(u - 1, 3)
        sum_step(u, 0)
        if u > 0:
            finish(u - 1)
        sum_step(u, 1)
    sum_step(NU - 1, 2)
    sum_step(NU - 1, 3)
    finish(NU - 1)

    for n in range(2):
        for d in range(2):
            wait(kv_part(s, n), kv_s.at[d, n])
        wait(kv_part(s, n), kv2_s.at[n])
    for n in range(4):
        wait(own_kv, kvc_s.at[n])
    for n in range(3):
        wait(ids_v.at[:, pl.ds(0, TOK)], sm_s.at[n])
        wait(gat_v.at[:, pl.ds(0, TOK)], sm_s.at[3 + n])
    wait(gain_mine, sm_s.at[6])
    wait(w_v.at[pl.ds(0, 3), pl.ds(0, WROWS), :], wa_s)
    wait(w_v.at[pl.ds(0, 12), pl.ds(0, WROWS), :], wb_s)
    wait(w_v.at[pl.ds(0, 15), pl.ds(0, WROWS), :], wc_s)
    for f in range(NF):
        wait(px_v.at[f], px_s.at[f])
        wait(s_v.at[f, pl.ds(0, FIFTEEN), :], dsp_s.at[f])
    for f in range(NR):
        wait(y_v.at[f, pl.ds(0, FIFTEEN), :], ret_s.at[f])
    wait(px2_v, px2_s)
    for d in range(2):
        wait(xg_v.at[pl.ds(0, 2), pl.ds(0, 7 * HALF_TOK), :], xg_s.at[d])
        for u in range(NU):
            for n in range(far(u, d)):
                wait(rs_s.at[u, d, n], rs_ss.at[u, d, n])

    @pl.when(giver == 0)
    def _():
        wait(wg_h, wk_s.at[0])
        wait(wu_h, wk_s.at[1])
        wait(wd_h, wk_s.at[2])

    @pl.when(giver == 1)
    def _():
        for n in range(8 + NR):
            wait(mine_chunks[n][1], wz_s.at[n])
            wait(mine_chunks[n][1], wf_s.at[n])


def per_device(
    q_rows, k_rows, value_rows, x_rows, out_weight, norm_gain, w_gate, w_up, w_down, expert_ids, gate_weights
):
    dma = pltpu.SemaphoreType.DMA
    any_spec = pl.BlockSpec(memory_space=pl.ANY)
    out = pl.pallas_call(
        layer_kernel,
        out_shape=jax.ShapeDtypeStruct((TOK, HALF_D), BF),
        in_specs=[any_spec] * 11,
        out_specs=pl.BlockSpec(memory_space=pltpu.VMEM),
        scratch_shapes=[
            pltpu.VMEM((TOK, D), BF),
            pltpu.VMEM((TOK, D), BF),
            pltpu.VMEM((8, 2, TOK, 256), BF),
            pltpu.VMEM((NP, D, 128), BF),
            pltpu.VMEM((1, D), F32),
            pltpu.VMEM((8, TOKS), jnp.int32),
            pltpu.VMEM((8, TOKS), F32),
            pltpu.VMEM((TOK, D), BF),
            pltpu.VMEM((NF, TOK, FC), BF),
            pltpu.VMEM((NF, HALF_TOK, FC), BF),
            pltpu.VMEM((2, HALF_TOK, FC), BF),
            pltpu.VMEM((NF, HALF_TOK, FC), F32),
            pltpu.VMEM((2, TOK, FC), F32),
            pltpu.VMEM((NF, TOKS, FC), BF),
            pltpu.VMEM((ROWS, TOKS), BF),
            pltpu.VMEM((ROWS, TOKS), F32),
            pltpu.VMEM((TOKS, ROWS), BF),
            pltpu.VMEM((NF, ROWS, FC), BF),
            pltpu.VMEM((NF, ROWS, FC), BF),
            pltpu.VMEM((D, FF), BF),
            pltpu.VMEM((D, FF), BF),
            pltpu.VMEM((FF, D), BF),
            pltpu.VMEM((ROWS, FF), F32),
            pltpu.VMEM((ROWS, FF), F32),
            pltpu.VMEM((ROWS, FF), BF),
            pltpu.VMEM((NR, ROWS, RC), BF),
            pltpu.VMEM((NR, ROWS, RC), BF),
            pltpu.VMEM((NR, TOKS, RC), F32),
            pltpu.VMEM((NU, 2, 4, TOK, RC), BF),
            pltpu.VMEM((NU, 2, 4, TOK, RC), BF),
            dma((8,)), dma((3,)), dma((8 + NR,)), dma((8 + NR,)), dma((3,)), dma((8 + NR,)),
            dma((2, 2)), dma((2, 2)), dma((4,)), dma((4,)), dma((2,)), dma((2,)),
            dma((7,)), dma((7,)),
            dma, dma((2,)), dma((2,)), dma, dma((4, 2)), dma((4, 2)), dma, dma,
            dma((NF,)), dma((NF,)), dma, dma,
            dma((2,)), dma((NF, 2, 4)), dma((NF,)), dma((NF,)), dma((NF,)), dma((NR,)), dma((NR,)), dma((NR,)),
            dma((NU, 2, 4)), dma((NU, 2, 4)),
        ],
        compiler_params=pltpu.CompilerParams(
            collective_id=0, has_side_effects=True, vmem_limit_bytes=62 * 1024 * 1024
        ),
        name="layer",
    )(
        q_rows[0],
        k_rows[0],
        value_rows[0],
        x_rows[0],
        out_weight,
        norm_gain.reshape(1, HALF_D),
        w_gate[0],
        w_up[0],
        w_down[0],
        expert_ids[0].T,
        gate_weights[0].T,
    )
    return out[None]


def solution(mesh):
    return jax.shard_map(
        per_device,
        mesh=mesh,
        in_specs=(
            P("expert", "seq", "tensor"),
            P("expert", "seq", "tensor"),
            P("expert", "seq", "tensor"),
            P("expert", "seq", None),
            P("tensor", "expert"),
            P("tensor"),
            P(("seq", "expert"), None, "tensor"),
            P(("seq", "expert"), None, "tensor"),
            P(("seq", "expert"), "tensor", None),
            P("expert", "seq", None),
            P("expert", "seq", None),
        ),
        out_specs=P("expert", "seq", "tensor"),
        check_vma=False,
    )
```

```python
import math

import jax
import jax.numpy as jnp
from jax import lax
from jax.experimental import pallas as pl
from jax.experimental.pallas import tpu as pltpu
from jax.sharding import PartitionSpec as P

MESH = pl.DeviceIdType.MESH
BF = jnp.bfloat16
F32 = jnp.float32

NX, NY, NZ = 4, 4, 8
NP = NX * NY
HEAD = 128
TOK = 128
HALF_TOK = 64
D = 2048
CAP = 12
NBLK = 4
MSG = NBLK * CAP
ROWS = NP * MSG
TOKS = NBLK * TOK
FFH = 384
FF = 768
HALF_D = D // 2
WROWS = 1024


def starts(widths):
    return tuple(sum(widths[:n]) for n in range(len(widths)))


CW = (256, 512, 512, 512, 256)
CS = starts(CW)
NF = len(CW)
RW = (256, 256, 256, 128, 128)
RING_U = 4
RS = starts(RW)
NU = len(RW)
PIECE = 256
GU = 2 * (D // PIECE)
SWAPS = GU + 2 * NU
PAIRS = tuple((u, h) for u in range(NU) for h in range(2))


def layer_kernel(
    q_h, k_h, v_h, x_h, w_h, gain_h, wg_h, wu_h, wd_h, ids_h, gat_h,
    out_ref,
    q_v, x_v, kv_v, w_v, gain_v, ids_v, gat_v,
    attn_v, ph_v, px_v, px2_v, mix_v, mixo_v,
    xg_v, p_v, gt_v, g_v, s_v, r_v,
    wg_v, wu_v, wd_v, ag_v, au_v, hid_v,
    y_v, yr_v, o_v, rs_s, rs_r, ds_v, dr_v,
    loc, hk, hz, wz_s, wk_s, wf_s,
    kv_s, kv_r, kvc_s, kvc_r, kv2_s, kv2_r,
    sm_s, sm_r,
    wa_s, wa_r, wa2_r, wb_s, wb_r, wb2_r, wc_s, wc_r,
    px_s, px_r, px2_s, px2_r,
    xg_s, xg_r, dsp_s, dsp_r, dsp_l, ret_s, ret_r, ret_l,
    rs_ss, rs_rs, ds_s, ds_r,
):
    rem, div = lax.rem, lax.div
    s = lax.axis_index("seq")
    e = lax.axis_index("expert")
    t = lax.axis_index("tensor")
    zh = div(s, 2)
    c = rem(s, 2)
    z = zh * 2 + t
    y = div(e, NX)
    x = rem(e, NX)
    oc = 1 - c
    giver = rem(c + t, 2)

    def dev(zz, ee, cc):
        return (div(zz, 2) * 2 + cc, ee, rem(zz, 2))

    def zmod(v):
        return rem(v + NZ, NZ)

    def send(src, dst, ss, rs, who):
        cp = pltpu.make_async_remote_copy(
            src_ref=src, dst_ref=dst, send_sem=ss, recv_sem=rs, device_id=who, device_id_type=MESH
        )
        cp.start()

    def local(src, dst, sem):
        pltpu.make_async_copy(src, dst, sem).start()

    def wait(ref, sem):
        pltpu.make_async_copy(ref, ref, sem).wait()

    def m8(v, n):
        return pl.multiple_of(v, n)

    other = dev(z, e, oc)
    partner = dev(z + 1 - 2 * t, e, c)
    cross = dev(z + 1 - 2 * t, e, oc)
    z_next, z_prev = dev(zmod(z + 1), e, c), dev(zmod(z - 1), e, c)
    zh_next, zh_prev = dev(zmod(z + 2), e, c), dev(zmod(z - 2), e, c)
    zh_opp = dev(zmod(z + 4), e, c)

    def plane_peer(k):
        return rem(y + div(k, NX), NY) * NX + rem(x + rem(k, NX), NX)

    a = (1 - c) * x + c * y
    b = (1 - c) * y + c * x

    def blk(ao, bo):
        aa, bb = rem(a + ao, 4), rem(b + bo, 4)
        return (1 - c) * (bb * 4 + aa) + c * (aa * 4 + bb)

    def frame_dev(ao, bo):
        return dev(z, blk(ao, bo), c)

    wrow = m8(c * WROWS, WROWS)
    a_next, a_prev = frame_dev(1, 0), frame_dev(3, 0)
    b_next, b_prev = frame_dev(0, 1), frame_dev(0, 3)
    OFF = (0, 3, 1, 2)

    own_kv = kv_v.at[s]
    local(k_h, kv_v.at[s, 0], loc.at[0])
    local(v_h, kv_v.at[s, 1], loc.at[1])
    local(w_h, w_v.at[e], loc.at[2])
    local(q_h, q_v, loc.at[3])
    local(x_h, x_v, loc.at[4])
    gcol = m8(t * HALF_D, HALF_D)
    local(gain_h, gain_v.at[:, pl.ds(gcol, HALF_D)], loc.at[5])
    icol = m8(zh * TOK, TOK)
    local(ids_h, ids_v.at[:, pl.ds(icol, TOK)], loc.at[6])
    local(gat_h, gat_v.at[:, pl.ds(icol, TOK)], loc.at[7])

    barrier = pltpu.get_barrier_semaphore()

    def greet(who):
        pl.semaphore_signal(barrier, inc=1, device_id=who, device_id_type=MESH)

    for who in (other, cross):
        greet(who)
    for k in range(1, NZ):
        greet(dev(zmod(z + k), e, c))

    def greet_plane(k, carry):
        greet(dev(z, plane_peer(k), c))
        return carry

    lax.fori_loop(1, NP, greet_plane, 0)
    wait(kv_v.at[s, 0], loc.at[0])
    wait(kv_v.at[s, 1], loc.at[1])
    wait(w_v.at[e], loc.at[2])
    wait(gain_v.at[:, pl.ds(gcol, HALF_D)], loc.at[5])
    wait(ids_v.at[:, pl.ds(icol, TOK)], loc.at[6])
    wait(gat_v.at[:, pl.ds(icol, TOK)], loc.at[7])
    pl.semaphore_wait(barrier, 2 + NZ - 1 + NP - 1)

    def kv_part(i, n):
        return kv_v.at[i, n]

    for n in range(2):
        send(kv_part(s, n), kv_part(s, n), kv_s.at[0, n], kv_r.at[0, n], zh_next)
        send(kv_part(s, 1 - n), kv_part(s, 1 - n), kv_s.at[1, 1 - n], kv_r.at[1, 1 - n], zh_prev)
    send(own_kv, own_kv, kvc_s.at[0], kvc_r.at[0], other)
    for n, who in enumerate((zh_next, zh_prev, zh_opp)):
        ids_mine = ids_v.at[:, pl.ds(icol, TOK)]
        gat_mine = gat_v.at[:, pl.ds(icol, TOK)]
        send(ids_mine, ids_mine, sm_s.at[n], sm_r.at[n], who)
        send(gat_mine, gat_mine, sm_s.at[3 + n], sm_r.at[3 + n], who)
    gain_mine = gain_v.at[:, pl.ds(gcol, HALF_D)]
    send(gain_mine, gain_mine, sm_s.at[6], sm_r.at[6], partner)

    def wpart(i, row0, rows):
        return w_v.at[i, pl.ds(m8(wrow + row0, 512), rows), :]

    mine = wpart(blk(0, 0), 0, WROWS)
    send(mine, mine, wa_s, wa_r.at[0], a_next)
    send(mine, mine, wa_s, wa_r.at[1], a_prev)
    send(mine, mine, wb_s, wb_r.at[0, 0], b_next)
    send(mine, mine, wb_s, wb_r.at[0, 1], b_prev)

    def on_chip(n, m):
        part = wpart(blk(OFF[n], OFF[m]), 0, WROWS)
        send(part, part, wc_s, wc_r.at[n, m], other)

    def spread_b(n):
        part = wpart(blk(OFF[n], 0), 0, WROWS)
        send(part, part, wb_s, wb_r.at[n, 0], b_next)
        send(part, part, wb_s, wb_r.at[n, 1], b_prev)

    hcol = m8(t * FFH, 128)
    gcolz = m8((1 - t) * FFH, 128)

    @pl.when(giver == 0)
    def _():
        for n, (src, dst) in enumerate(
            (
                (wg_h, wg_v.at[:, pl.ds(hcol, FFH)]),
                (wu_h, wu_v.at[:, pl.ds(hcol, FFH)]),
                (wd_h, wd_v.at[pl.ds(hcol, FFH), :]),
            )
        ):
            local(src, dst, hk.at[n])
            send(src, dst, wk_s.at[n], hk.at[n], other)

    left = rem(zh + 3, 4) * 2 + c
    right = rem(zh + 1, 4) * 2 + c
    opp = rem(zh + 2, 4) * 2 + c
    wait(kv_part(left, 0), kv_r.at[0, 0])
    send(kv_part(left, 0), kv_part(left, 0), kv2_s.at[0], kv2_r.at[0], zh_next)
    wait(kv_part(right, 1), kv_r.at[1, 1])
    send(kv_part(right, 1), kv_part(right, 1), kv2_s.at[1], kv2_r.at[1], zh_prev)

    wait(mine, wa_r.at[0])
    part = wpart(blk(3, 0), 0, 512)
    send(part, part, wa_s, wa2_r.at[0], a_next)
    wait(mine, wa_r.at[1])
    part = wpart(blk(1, 0), 512, 512)
    send(part, part, wa_s, wa2_r.at[1], a_prev)
    spread_b(1)
    spread_b(2)
    on_chip(1, 0)
    on_chip(2, 0)

    wait(kv_part(left, 1), kv_r.at[0, 1])
    send(kv_v.at[left], kv_v.at[left], kvc_s.at[1], kvc_r.at[1], other)
    wait(kv_part(right, 0), kv_r.at[1, 0])
    send(kv_v.at[right], kv_v.at[right], kvc_s.at[2], kvc_r.at[2], other)

    def wchunks(h):
        col = m8(h * FFH, 128)
        out = []
        for lo in range(0, D, PIECE):
            rows = pl.ds(lo, PIECE)
            out.append((wg_h.at[rows, :], wg_v.at[rows, pl.ds(col, FFH)]))
            out.append((wu_h.at[rows, :], wu_v.at[rows, pl.ds(col, FFH)]))
        for u, h in PAIRS:
            cols = pl.ds(h * HALF_D + RS[u], RW[u])
            out.append((wd_h.at[:, cols], wd_v.at[pl.ds(col, FFH), cols]))
        return out

    mine_chunks = wchunks(t)
    their_chunks = wchunks(1 - t)

    def swap(lo, hi):
        @pl.when(giver == 1)
        def _():
            for n in range(lo, hi):
                src, dst = mine_chunks[n]
                send(src, dst, wz_s.at[n], hz.at[n], cross)

    def weights_in(n):
        dst = their_chunks[n][1]
        wait(dst, hz.at[n])

        @pl.when(giver == 1)
        def _():
            send(dst, dst, wf_s.at[n], hz.at[n], other)

    wait(wpart(blk(2, 0), 0, 512), wa2_r.at[0])
    wait(wpart(blk(2, 0), 512, 512), wa2_r.at[1])
    spread_b(3)
    on_chip(3, 0)

    def second_axis(n):
        wait(mine, wb_r.at[n, 0])
        fwd = wpart(blk(OFF[n], 3), 0, 512)
        send(fwd, fwd, wb_s, wb2_r.at[n, 0], b_next)
        on_chip(n, 1)
        wait(mine, wb_r.at[n, 1])
        fwd = wpart(blk(OFF[n], 1), 512, 512)
        send(fwd, fwd, wb_s, wb2_r.at[n, 1], b_prev)
        on_chip(n, 2)

    def second_axis_end(n):
        wait(wpart(blk(OFF[n], 2), 0, 512), wb2_r.at[n, 0])
        wait(wpart(blk(OFF[n], 2), 512, 512), wb2_r.at[n, 1])
        on_chip(n, 3)

    second_axis(0)

    wait(kv_part(opp, 0), kv2_r.at[0])
    wait(kv_part(opp, 1), kv2_r.at[1])
    send(kv_v.at[opp], kv_v.at[opp], kvc_s.at[3], kvc_r.at[3], other)

    for n in range(3):
        wait(ids_v.at[:, pl.ds(icol, TOK)], sm_r.at[n])
        wait(gat_v.at[:, pl.ds(icol, TOK)], sm_r.at[3 + n])
    ids = ids_v[...]
    gates = gat_v[...]
    mine_ids = NP * z + lax.broadcasted_iota(jnp.int32, (NP, TOKS), 0)
    member = jnp.zeros((NP, TOKS), F32)
    gate_of = jnp.zeros((NP, TOKS), F32)
    for k in range(8):
        hit = ids[k : k + 1, :] == mine_ids
        member = jnp.where(hit, 1.0, member)
        gate_of = jnp.where(hit, gates[k : k + 1, :], gate_of)
    before = (
        lax.broadcasted_iota(jnp.int32, (TOK, TOK), 0) < lax.broadcasted_iota(jnp.int32, (TOK, TOK), 1)
    ).astype(BF)
    places = []
    for n in range(NBLK):
        mb = member[:, n * TOK : (n + 1) * TOK]
        rank = jnp.dot(mb.astype(BF), before, preferred_element_type=F32)
        places.append(jnp.where(mb > 0.5, rank + float(n * CAP), -1.0))
    place = jnp.concatenate(places, axis=1)
    row_id = lax.broadcasted_iota(jnp.int32, (MSG, TOKS), 0).astype(F32)
    for j in range(NP):
        hit = jnp.broadcast_to(place[j : j + 1, :], (MSG, TOKS)) == row_id
        p_v[j * MSG : (j + 1) * MSG, :] = jnp.where(hit, 1.0, 0.0).astype(BF)
        gt_v[j * MSG : (j + 1) * MSG, :] = jnp.where(
            hit, jnp.broadcast_to(gate_of[j : j + 1, :], (MSG, TOKS)), 0.0
        )
    for j in range(ROWS // 128):
        g_v[:, j * 128 : (j + 1) * 128] = gt_v[j * 128 : (j + 1) * 128, :].T.astype(BF)

    second_axis(1)
    for n in range(4):
        wait(own_kv, kvc_r.at[n])
    wait(q_v, loc.at[3])
    softmax_scale = 1.0 / math.sqrt(HEAD)
    allowed = lax.broadcasted_iota(jnp.int32, (2 * TOK, 8 * TOK), 1) <= (
        s * TOK + rem(lax.broadcasted_iota(jnp.int32, (2 * TOK, 8 * TOK), 0), TOK)
    )

    def heads_pair(i, carry):
        g = div(i, 4)
        lane = m8(i * 256, 256)
        kl = m8(g * HEAD, HEAD)
        qq = jnp.concatenate(
            [q_v[:, pl.ds(lane, HEAD)], q_v[:, pl.ds(m8(lane + HEAD, HEAD), HEAD)]], axis=0
        )
        kk = kv_v[:, 0, :, pl.ds(kl, HEAD)].reshape(8 * TOK, HEAD)
        vv = kv_v[:, 1, :, pl.ds(kl, HEAD)].reshape(8 * TOK, HEAD)
        sc = lax.dot_general(qq, kk, (((1,), (1,)), ((), ())), preferred_element_type=F32)
        sc = jnp.where(allowed, sc * softmax_scale, -1e30)
        top = jnp.max(sc, axis=1, keepdims=True)
        p = jnp.exp(sc - top)
        tot = jnp.sum(p, axis=1, keepdims=True)
        o = jnp.dot(p.astype(BF), vv, preferred_element_type=F32) / tot
        o = o.astype(BF)
        attn_v[:, pl.ds(lane, HEAD)] = o[:TOK]
        attn_v[:, pl.ds(m8(lane + HEAD, HEAD), HEAD)] = o[TOK:]
        return carry

    for grp in range(4):
        lax.fori_loop(2 * grp, 2 * grp + 2, heads_pair, 0)
        if grp == 0:
            second_axis(2)
        if grp == 1:
            second_axis_end(0)
            second_axis(3)
        if grp == 2:
            second_axis_end(1)

    my_row = m8(t * HALF_TOK, HALF_TOK)
    their_row = m8((1 - t) * HALF_TOK, HALF_TOK)

    def project(n, m):
        i = blk(OFF[n], OFF[m])
        if n + m > 0:
            wait(mine, wc_r.at[m, n])
        ph_v[i] = jnp.dot(attn_v[...], w_v[i], preferred_element_type=F32).astype(BF)
        send(ph_v.at[i, pl.ds(their_row, HALF_TOK), :], px_v.at[i], px_s, px_r, partner)

    for n in range(3):
        for m in range(3):
            project(n, m)
    project(3, 0)
    project(0, 3)
    project(1, 3)
    project(3, 1)
    second_axis_end(2)
    project(2, 3)
    project(3, 2)
    second_axis_end(3)
    project(3, 3)
    swap(0, 2)
    wait(x_v, loc.at[4])
    wait(gain_v.at[:, pl.ds(gcol, HALF_D)], sm_r.at[6])
    wait(px_v, px_r)
    power = jnp.zeros((HALF_TOK, 1), F32)
    for i in range(NP):
        mix = (
            x_v[pl.ds(my_row, HALF_TOK), i * 128 : (i + 1) * 128].astype(F32)
            + ph_v[i, pl.ds(my_row, HALF_TOK), :].astype(F32)
            + px_v[i].astype(F32)
        )
        mix_v[:, i * 128 : (i + 1) * 128] = mix
        power = power + jnp.sum(mix * mix, axis=1, keepdims=True)
    inverse = lax.rsqrt(power / D + 1e-06)

    zrow = m8(z * HALF_TOK, HALF_TOK)
    def cols_of(f):
        return pl.ds(CS[f], CW[f])

    def ring_open(f):
        cols = cols_of(f)
        xg_v[pl.ds(zrow, HALF_TOK), cols] = (mix_v[:, cols] * inverse * gain_v[:, cols]).astype(BF)
        shard = xg_v.at[pl.ds(zrow, HALF_TOK), cols]
        send(shard, shard, xg_s.at[f, 0], xg_r.at[f, 0, 0], z_next)
        send(shard, shard, xg_s.at[f, 1], xg_r.at[f, 1, 0], z_prev)

    def reach(f, d):
        return 4 if (f + d) % 2 == 0 else 3

    def ring_step(f, k):
        for d in range(2):
            if k > reach(f, d):
                continue
            src_z = zmod(z - k) if d == 0 else zmod(z + k)
            shard = xg_v.at[pl.ds(m8(src_z * HALF_TOK, HALF_TOK), HALF_TOK), cols_of(f)]
            wait(shard, xg_r.at[f, d, k - 1])
            if k + 1 <= reach(f, d):
                send(shard, shard, xg_s.at[f, d], xg_r.at[f, d, k], z_next if d == 0 else z_prev)

    my_slot = pl.ds(m8(e * MSG, 16), MSG)

    def exchange(buf, dst, cols, ss, rs, ls, lo, hi):
        def one(k, carry):
            peer = plane_peer(k)
            send(
                buf.at[pl.ds(m8(peer * MSG, 16), MSG), cols],
                dst.at[my_slot, cols],
                ss,
                rs,
                dev(z, peer, c),
            )
            return carry

        parts = hi - lo + 1
        for n in range(parts):
            lax.fori_loop(1 + n * (NP - 1) // parts, 1 + (n + 1) * (NP - 1) // parts, one, 0)
            if n < parts - 1:
                swap(lo + n, lo + n + 1)
        local(buf.at[my_slot, cols], dst.at[my_slot, cols], ls)

    FIFTEEN = pl.ds(0, (NP - 1) * MSG)

    def exchanged(dst, cols, rs, ls):
        wait(dst.at[FIFTEEN, cols], rs)
        wait(dst.at[my_slot, cols], ls)

    def pick_rows(f):
        cols = cols_of(f)

        def group(i, carry):
            rows = pl.ds(m8(i * 256, 256), 256)
            s_v[rows, cols] = jnp.dot(p_v[rows, :], xg_v[:, cols], preferred_element_type=F32).astype(BF)
            return carry

        lax.fori_loop(0, ROWS // 256, group, 0)
        lo, hi = ((2, 4), (4, 8), (8, 12), (12, GU), (GU, GU + 2))[f]
        exchange(s_v, r_v, cols, dsp_s.at[f], dsp_r.at[f], dsp_l.at[f], lo, hi)

    ring_open(0)
    ring_open(1)
    for wave in range(1, NF + 4):
        for f in range(NF):
            if 1 <= wave - f <= 4:
                ring_step(f, wave - f)
        if wave + 1 < NF:
            ring_open(wave + 1)
        if wave >= 4:
            pick_rows(wave - 4)
    mid = ph_v.at[pl.ds((1 - t) * 8, 8), pl.ds(my_row, HALF_TOK), :]
    send(mid, px2_v, px2_s, px2_r, partner)

    wait(wg_v.at[:, pl.ds(hcol, FFH)], hk.at[0])
    wait(wu_v.at[:, pl.ds(hcol, FFH)], hk.at[1])
    for f in range(NF):
        for n in range(2 * (CS[f] // PIECE), 2 * ((CS[f] + CW[f]) // PIECE)):
            weights_in(n)
        exchanged(r_v, cols_of(f), dsp_r.at[f], dsp_l.at[f])
        lo, hi = CS[f], CS[f] + CW[f]

        def gate_up(i, carry):
            rows = pl.ds(m8(i * 256, 256), 256)
            rr = r_v[rows, lo:hi]
            ga = jnp.dot(rr, wg_v[lo:hi, :], preferred_element_type=F32)
            ua = jnp.dot(rr, wu_v[lo:hi, :], preferred_element_type=F32)
            if f > 0:
                ga = ga + ag_v[rows, :]
                ua = ua + au_v[rows, :]
            if f < NF - 1:
                ag_v[rows, :] = ga
                au_v[rows, :] = ua
            else:
                hid_v[rows, :] = (ga / (1.0 + jnp.exp(-ga)) * ua).astype(BF)
            return carry

        lax.fori_loop(0, ROWS // 256, gate_up, 0)

    wait(wd_v.at[pl.ds(hcol, FFH), :], hk.at[2])
    def pair_cols(u, h):
        return pl.ds(h * HALF_D + RS[u], RW[u])

    def down(n):
        u, h = PAIRS[n]
        weights_in(GU + n)
        cols = pair_cols(u, h)

        def group(i, carry):
            rows = pl.ds(m8(i * 256, 256), 256)
            y0 = jnp.dot(hid_v[rows, :FFH], wd_v[:FFH, cols], preferred_element_type=F32)
            y1 = jnp.dot(hid_v[rows, FFH:], wd_v[FFH:, cols], preferred_element_type=F32)
            y_v[rows, cols] = (y0.astype(BF).astype(F32) + y1.astype(BF).astype(F32)).astype(BF)
            return carry

        lax.fori_loop(0, ROWS // 256, group, 0)

    def give_back(n):
        u, h = PAIRS[n]
        lo = GU + n + 2
        hi = min(lo + 1, SWAPS)
        lo = min(lo, hi)
        exchange(y_v, yr_v, pair_cols(u, h), ret_s.at[u, h], ret_r.at[u, h], ret_l.at[u, h], lo, hi)

    down(0)
    give_back(0)
    down(1)
    give_back(1)

    wait(px2_v, px2_r)
    mixo_v[pl.ds(my_row, HALF_TOK), :] = mix_v[:, pl.ds(gcol, HALF_D)]
    for i in range(8):
        cols = pl.ds(m8(gcol + i * 128, 128), 128)
        mixo_v[pl.ds(their_row, HALF_TOK), i * 128 : (i + 1) * 128] = (
            x_v[pl.ds(their_row, HALF_TOK), cols].astype(F32)
            + ph_v[t * 8 + i, pl.ds(their_row, HALF_TOK), :].astype(F32)
            + px2_v[i].astype(F32)
        )

    def combine(u, h):
        cols = pair_cols(u, h)
        exchanged(yr_v, cols, ret_r.at[u, h], ret_l.at[u, h])

        def group(i, carry):
            rows = pl.ds(m8(i * 256, 256), 256)
            o_v[rows, cols] = jnp.dot(g_v[rows, :], yr_v[:, cols], preferred_element_type=F32)
            return carry

        lax.fori_loop(0, TOKS // 256, group, 0)

    def own_part(dest, u):
        cols = pl.ds(m8(rem(dest, 2) * HALF_D + RS[u], 128), RW[u])
        return o_v[pl.ds(m8(div(dest, 2) * TOK, TOK), TOK), cols]

    def far(u, d):
        return 4 if (u + d) % 2 == 0 else 3

    def sum_step(u, i):
        cols = pl.ds(RS[u], RW[u])
        for d in range(2):
            dist = far(u, d) - i
            if dist < 1:
                continue
            dest = zmod(z + dist) if d == 0 else zmod(z - dist)
            part = own_part(dest, u)
            if i > 0:
                wait(rs_r.at[d, dist, :, cols], rs_rs.at[u, d, dist])
                part = part + rs_r[d, dist, :, cols].astype(F32)
            rs_s[d, dist - 1, :, cols] = part.astype(BF)
            send(
                rs_s.at[d, dist - 1, :, cols],
                rs_r.at[d, dist - 1, :, cols],
                rs_ss.at[u, d, dist - 1],
                rs_rs.at[u, d, dist - 1],
                z_next if d == 0 else z_prev,
            )

    FAR_FIRST = (4, 3, 5, 2, 6, 1, 7)

    def send_sums(u):
        for k in FAR_FIRST:
            dest = zmod(z + k)
            ds_v[u - RING_U, k - 1] = own_part(dest, u).astype(BF)
            send(
                ds_v.at[u - RING_U, k - 1],
                dr_v.at[u - RING_U, k - 1],
                ds_s.at[u - RING_U],
                ds_r.at[u - RING_U],
                dev(dest, e, c),
            )

    def finish(u):
        cols = pl.ds(RS[u], RW[u])
        total = own_part(z, u)
        if u < RING_U:
            for d in range(2):
                wait(rs_r.at[d, 0, :, cols], rs_rs.at[u, d, 0])
                total = total + rs_r[d, 0, :, cols].astype(F32)
        else:
            wait(dr_v.at[u - RING_U], ds_r.at[u - RING_U])
            for k in range(NZ - 1):
                total = total + dr_v[u - RING_U, k].astype(F32)
        out_ref[:, cols] = (mixo_v[:, cols] + total).astype(BF)

    last = 2 * NU
    for n in range(2, last + 4):
        if n < last:
            down(n)
        if n - 2 < last:
            combine(*PAIRS[n - 2])
        for u in range(NU):
            i = n - (2 * u + 3)
            if u >= RING_U:
                if i == 0:
                    send_sums(u)
            elif 0 <= i < 4:
                sum_step(u, i)
            elif i == 4:
                finish(u)
        if n < last:
            give_back(n)
    for u in range(RING_U, NU):
        finish(u)

    for n in range(2):
        for d in range(2):
            wait(kv_part(s, n), kv_s.at[d, n])
        wait(kv_part(s, n), kv2_s.at[n])
    for n in range(4):
        wait(own_kv, kvc_s.at[n])
    for n in range(3):
        wait(ids_v.at[:, pl.ds(0, TOK)], sm_s.at[n])
        wait(gat_v.at[:, pl.ds(0, TOK)], sm_s.at[3 + n])
    wait(gain_mine, sm_s.at[6])
    wait(w_v.at[pl.ds(0, 3), pl.ds(0, WROWS), :], wa_s)
    wait(w_v.at[pl.ds(0, 12), pl.ds(0, WROWS), :], wb_s)
    wait(w_v.at[pl.ds(0, 15), pl.ds(0, WROWS), :], wc_s)
    wait(px_v, px_s)
    for f in range(NF):
        wait(s_v.at[FIFTEEN, cols_of(f)], dsp_s.at[f])
        for d in range(2):
            wait(xg_v.at[pl.ds(0, reach(f, d) * HALF_TOK), cols_of(f)], xg_s.at[f, d])
    wait(px2_v, px2_s)
    for u in range(NU):
        for h in range(2):
            wait(y_v.at[FIFTEEN, pair_cols(u, h)], ret_s.at[u, h])
        for d in range(2):
            for n in range(far(u, d) if u < RING_U else 0):
                wait(rs_s.at[d, n, :, pl.ds(RS[u], RW[u])], rs_ss.at[u, d, n])
        if u >= RING_U:
            wait(ds_v.at[u - RING_U], ds_s.at[u - RING_U])

    @pl.when(giver == 0)
    def _():
        wait(wg_h, wk_s.at[0])
        wait(wu_h, wk_s.at[1])
        wait(wd_h, wk_s.at[2])

    @pl.when(giver == 1)
    def _():
        for n in range(SWAPS):
            wait(mine_chunks[n][1], wz_s.at[n])
            wait(mine_chunks[n][1], wf_s.at[n])


def per_device(
    q_rows, k_rows, value_rows, x_rows, out_weight, norm_gain, w_gate, w_up, w_down, expert_ids, gate_weights
):
    dma = pltpu.SemaphoreType.DMA
    any_spec = pl.BlockSpec(memory_space=pl.ANY)
    out = pl.pallas_call(
        layer_kernel,
        out_shape=jax.ShapeDtypeStruct((TOK, HALF_D), BF),
        in_specs=[any_spec] * 11,
        out_specs=pl.BlockSpec(memory_space=pltpu.VMEM),
        scratch_shapes=[
            pltpu.VMEM((TOK, D), BF),
            pltpu.VMEM((TOK, D), BF),
            pltpu.VMEM((8, 2, TOK, 256), BF),
            pltpu.VMEM((NP, D, 128), BF),
            pltpu.VMEM((1, D), F32),
            pltpu.VMEM((8, TOKS), jnp.int32),
            pltpu.VMEM((8, TOKS), F32),
            pltpu.VMEM((TOK, D), BF),
            pltpu.VMEM((NP, TOK, 128), BF),
            pltpu.VMEM((NP, HALF_TOK, 128), BF),
            pltpu.VMEM((8, HALF_TOK, 128), BF),
            pltpu.VMEM((HALF_TOK, D), F32),
            pltpu.VMEM((TOK, HALF_D), F32),
            pltpu.VMEM((TOKS, D), BF),
            pltpu.VMEM((ROWS, TOKS), BF),
            pltpu.VMEM((ROWS, TOKS), F32),
            pltpu.VMEM((TOKS, ROWS), BF),
            pltpu.VMEM((ROWS, D), BF),
            pltpu.VMEM((ROWS, D), BF),
            pltpu.VMEM((D, FF), BF),
            pltpu.VMEM((D, FF), BF),
            pltpu.VMEM((FF, D), BF),
            pltpu.VMEM((ROWS, FF), F32),
            pltpu.VMEM((ROWS, FF), F32),
            pltpu.VMEM((ROWS, FF), BF),
            pltpu.VMEM((ROWS, D), BF),
            pltpu.VMEM((ROWS, D), BF),
            pltpu.VMEM((TOKS, D), F32),
            pltpu.VMEM((2, 4, TOK, HALF_D), BF),
            pltpu.VMEM((2, 4, TOK, HALF_D), BF),
            pltpu.VMEM((NU - RING_U, NZ - 1, TOK, 128), BF),
            pltpu.VMEM((NU - RING_U, NZ - 1, TOK, 128), BF),
            dma((8,)), dma((3,)), dma((SWAPS,)), dma((SWAPS,)), dma((3,)), dma((SWAPS,)),
            dma((2, 2)), dma((2, 2)), dma((4,)), dma((4,)), dma((2,)), dma((2,)),
            dma((7,)), dma((7,)),
            dma, dma((2,)), dma((2,)), dma, dma((4, 2)), dma((4, 2)), dma, dma((4, 4)),
            dma, dma, dma, dma,
            dma((NF, 2)), dma((NF, 2, 4)), dma((NF,)), dma((NF,)), dma((NF,)),
            dma((NU, 2)), dma((NU, 2)), dma((NU, 2)),
            dma((NU, 2, 4)), dma((NU, 2, 4)), dma((NU - RING_U,)), dma((NU - RING_U,)),
        ],
        compiler_params=pltpu.CompilerParams(
            collective_id=0, has_side_effects=True, vmem_limit_bytes=62 * 1024 * 1024
        ),
        name="layer",
    )(
        q_rows[0],
        k_rows[0],
        value_rows[0],
        x_rows[0],
        out_weight,
        norm_gain.reshape(1, HALF_D),
        w_gate[0],
        w_up[0],
        w_down[0],
        expert_ids[0].T,
        gate_weights[0].T,
    )
    return out[None]


def solution(mesh):
    return jax.shard_map(
        per_device,
        mesh=mesh,
        in_specs=(
            P("expert", "seq", "tensor"),
            P("expert", "seq", "tensor"),
            P("expert", "seq", "tensor"),
            P("expert", "seq", None),
            P("tensor", "expert"),
            P("tensor"),
            P(("seq", "expert"), None, "tensor"),
            P(("seq", "expert"), None, "tensor"),
            P(("seq", "expert"), "tensor", None),
            P("expert", "seq", None),
            P("expert", "seq", None),
        ),
        out_specs=P("expert", "seq", "tensor"),
        check_vma=False,
    )
```

```python
import math

import jax
import jax.numpy as jnp
from jax import lax
from jax.experimental import pallas as pl
from jax.experimental.pallas import tpu as pltpu
from jax.sharding import PartitionSpec as P

MESH = pl.DeviceIdType.MESH
BF = jnp.bfloat16
F32 = jnp.float32

NX, NY, NZ = 4, 4, 8
NP = NX * NY
HEAD = 128
TOK = 128
HALF_TOK = 64
D = 2048
CAP = 12
NBLK = 4
MSG = NBLK * CAP
ROWS = NP * MSG
TOKS = NBLK * TOK
FFH = 384
FF = 768
HALF_D = D // 2
WROWS = 1024


def starts(widths):
    return tuple(sum(widths[:n]) for n in range(len(widths)))


CW = (256, 512, 512, 512, 256)
CS = starts(CW)
NF = len(CW)
RW = (128, 256, 256, 256, 128)
RING_U = 4
RS = starts(RW)
NU = len(RW)
PIECE = 256
GU = 2 * (D // PIECE)
SWAPS = GU + 2 * NU
PAIRS = tuple((u, h) for u in range(NU) for h in range(2))


def layer_kernel(
    q_h, k_h, v_h, x_h, w_h, gain_h, wg_h, wu_h, wd_h, ids_h, gat_h,
    out_ref,
    q_v, x_v, kv_v, w_v, gain_v, ids_v, gat_v,
    attn_v, ph_v, px_v, px2_v, mix_v, mixo_v,
    xg_v, p_v, gt_v, g_v, s_v, r_v,
    wg_v, wu_v, wd_v, ag_v, au_v, hid_v,
    y_v, yr_v, o_v, rs_s, rs_r, ds_v, dr_v,
    loc, hk, hz, wz_s, wk_s, wf_s,
    kv_s, kv_r, kvc_s, kvc_r, kv2_s, kv2_r,
    sm_s, sm_r,
    wa_s, wa_r, wa2_r, wb_s, wb_r, wb2_r, wc_s, wc_r,
    px_s, px_r, px2_s, px2_r,
    xg_s, xg_r, dsp_s, dsp_r, dsp_l, ret_s, ret_r, ret_l,
    rs_ss, rs_rs, ds_s, ds_r,
):
    rem, div = lax.rem, lax.div
    s = lax.axis_index("seq")
    e = lax.axis_index("expert")
    t = lax.axis_index("tensor")
    zh = div(s, 2)
    c = rem(s, 2)
    z = zh * 2 + t
    y = div(e, NX)
    x = rem(e, NX)
    oc = 1 - c
    giver = rem(c + t, 2)

    def dev(zz, ee, cc):
        return (div(zz, 2) * 2 + cc, ee, rem(zz, 2))

    def zmod(v):
        return rem(v + NZ, NZ)

    def send(src, dst, ss, rs, who):
        cp = pltpu.make_async_remote_copy(
            src_ref=src, dst_ref=dst, send_sem=ss, recv_sem=rs, device_id=who, device_id_type=MESH
        )
        cp.start()

    def local(src, dst, sem):
        pltpu.make_async_copy(src, dst, sem).start()

    def wait(ref, sem):
        pltpu.make_async_copy(ref, ref, sem).wait()

    def m8(v, n):
        return pl.multiple_of(v, n)

    other = dev(z, e, oc)
    partner = dev(z + 1 - 2 * t, e, c)
    cross = dev(z + 1 - 2 * t, e, oc)
    z_next, z_prev = dev(zmod(z + 1), e, c), dev(zmod(z - 1), e, c)
    zh_next, zh_prev = dev(zmod(z + 2), e, c), dev(zmod(z - 2), e, c)
    zh_opp = dev(zmod(z + 4), e, c)

    def plane_peer(k):
        return rem(y + div(k, NX), NY) * NX + rem(x + rem(k, NX), NX)

    a = (1 - c) * x + c * y
    b = (1 - c) * y + c * x

    def blk(ao, bo):
        aa, bb = rem(a + ao, 4), rem(b + bo, 4)
        return (1 - c) * (bb * 4 + aa) + c * (aa * 4 + bb)

    def frame_dev(ao, bo):
        return dev(z, blk(ao, bo), c)

    wrow = m8(c * WROWS, WROWS)
    a_next, a_prev = frame_dev(1, 0), frame_dev(3, 0)
    b_next, b_prev = frame_dev(0, 1), frame_dev(0, 3)
    OFF = (0, 3, 1, 2)

    own_kv = kv_v.at[s]
    local(k_h, kv_v.at[s, 0], loc.at[0])
    local(v_h, kv_v.at[s, 1], loc.at[1])
    local(w_h, w_v.at[e], loc.at[2])
    local(q_h, q_v, loc.at[3])
    local(x_h, x_v, loc.at[4])
    gcol = m8(t * HALF_D, HALF_D)
    local(gain_h, gain_v.at[:, pl.ds(gcol, HALF_D)], loc.at[5])
    icol = m8(zh * TOK, TOK)
    local(ids_h, ids_v.at[:, pl.ds(icol, TOK)], loc.at[6])
    local(gat_h, gat_v.at[:, pl.ds(icol, TOK)], loc.at[7])

    barrier = pltpu.get_barrier_semaphore()

    def greet(who):
        pl.semaphore_signal(barrier, inc=1, device_id=who, device_id_type=MESH)

    for who in (other, cross):
        greet(who)
    for k in range(1, NZ):
        greet(dev(zmod(z + k), e, c))

    def greet_plane(k, carry):
        greet(dev(z, plane_peer(k), c))
        return carry

    lax.fori_loop(1, NP, greet_plane, 0)
    wait(kv_v.at[s, 0], loc.at[0])
    wait(kv_v.at[s, 1], loc.at[1])
    wait(w_v.at[e], loc.at[2])
    wait(gain_v.at[:, pl.ds(gcol, HALF_D)], loc.at[5])
    wait(ids_v.at[:, pl.ds(icol, TOK)], loc.at[6])
    wait(gat_v.at[:, pl.ds(icol, TOK)], loc.at[7])
    pl.semaphore_wait(barrier, 2 + NZ - 1 + NP - 1)

    def kv_part(i, n):
        return kv_v.at[i, n]

    for n in range(2):
        send(kv_part(s, n), kv_part(s, n), kv_s.at[0, n], kv_r.at[0, n], zh_next)
        send(kv_part(s, 1 - n), kv_part(s, 1 - n), kv_s.at[1, 1 - n], kv_r.at[1, 1 - n], zh_prev)
    send(own_kv, own_kv, kvc_s.at[0], kvc_r.at[0], other)
    for n, who in enumerate((zh_next, zh_prev, zh_opp)):
        ids_mine = ids_v.at[:, pl.ds(icol, TOK)]
        gat_mine = gat_v.at[:, pl.ds(icol, TOK)]
        send(ids_mine, ids_mine, sm_s.at[n], sm_r.at[n], who)
        send(gat_mine, gat_mine, sm_s.at[3 + n], sm_r.at[3 + n], who)
    gain_mine = gain_v.at[:, pl.ds(gcol, HALF_D)]
    send(gain_mine, gain_mine, sm_s.at[6], sm_r.at[6], partner)

    def wpart(i, row0, rows):
        return w_v.at[i, pl.ds(m8(wrow + row0, 512), rows), :]

    mine = wpart(blk(0, 0), 0, WROWS)
    send(mine, mine, wa_s, wa_r.at[0], a_next)
    send(mine, mine, wa_s, wa_r.at[1], a_prev)
    send(mine, mine, wb_s, wb_r.at[0, 0], b_next)
    send(mine, mine, wb_s, wb_r.at[0, 1], b_prev)

    def on_chip(n, m):
        part = wpart(blk(OFF[n], OFF[m]), 0, WROWS)
        send(part, part, wc_s, wc_r.at[n, m], other)

    def spread_b(n):
        part = wpart(blk(OFF[n], 0), 0, WROWS)
        send(part, part, wb_s, wb_r.at[n, 0], b_next)
        send(part, part, wb_s, wb_r.at[n, 1], b_prev)

    hcol = m8(t * FFH, 128)
    gcolz = m8((1 - t) * FFH, 128)

    @pl.when(giver == 0)
    def _():
        for n, (src, dst) in enumerate(
            (
                (wg_h, wg_v.at[:, pl.ds(hcol, FFH)]),
                (wu_h, wu_v.at[:, pl.ds(hcol, FFH)]),
                (wd_h, wd_v.at[pl.ds(hcol, FFH), :]),
            )
        ):
            local(src, dst, hk.at[n])
            send(src, dst, wk_s.at[n], hk.at[n], other)

    left = rem(zh + 3, 4) * 2 + c
    right = rem(zh + 1, 4) * 2 + c
    opp = rem(zh + 2, 4) * 2 + c
    wait(kv_part(left, 0), kv_r.at[0, 0])
    send(kv_part(left, 0), kv_part(left, 0), kv2_s.at[0], kv2_r.at[0], zh_next)
    wait(kv_part(right, 1), kv_r.at[1, 1])
    send(kv_part(right, 1), kv_part(right, 1), kv2_s.at[1], kv2_r.at[1], zh_prev)

    wait(mine, wa_r.at[0])
    part = wpart(blk(3, 0), 0, 512)
    send(part, part, wa_s, wa2_r.at[0], a_next)
    wait(mine, wa_r.at[1])
    part = wpart(blk(1, 0), 512, 512)
    send(part, part, wa_s, wa2_r.at[1], a_prev)
    spread_b(1)
    spread_b(2)
    on_chip(1, 0)
    on_chip(2, 0)

    wait(kv_part(left, 1), kv_r.at[0, 1])
    send(kv_v.at[left], kv_v.at[left], kvc_s.at[1], kvc_r.at[1], other)
    wait(kv_part(right, 0), kv_r.at[1, 0])
    send(kv_v.at[right], kv_v.at[right], kvc_s.at[2], kvc_r.at[2], other)

    def wchunks(h):
        col = m8(h * FFH, 128)
        out = []
        for lo in range(0, D, PIECE):
            rows = pl.ds(lo, PIECE)
            out.append((wg_h.at[rows, :], wg_v.at[rows, pl.ds(col, FFH)]))
            out.append((wu_h.at[rows, :], wu_v.at[rows, pl.ds(col, FFH)]))
        for u, h in PAIRS:
            cols = pl.ds(h * HALF_D + RS[u], RW[u])
            out.append((wd_h.at[:, cols], wd_v.at[pl.ds(col, FFH), cols]))
        return out

    mine_chunks = wchunks(t)
    their_chunks = wchunks(1 - t)

    def swap(lo, hi):
        @pl.when(giver == 1)
        def _():
            for n in range(lo, hi):
                src, dst = mine_chunks[n]
                send(src, dst, wz_s.at[n], hz.at[n], cross)

    def weights_in(n):
        dst = their_chunks[n][1]
        wait(dst, hz.at[n])

        @pl.when(giver == 1)
        def _():
            send(dst, dst, wf_s.at[n], hz.at[n], other)

    wait(wpart(blk(2, 0), 0, 512), wa2_r.at[0])
    wait(wpart(blk(2, 0), 512, 512), wa2_r.at[1])
    spread_b(3)
    on_chip(3, 0)

    def second_axis(n):
        wait(mine, wb_r.at[n, 0])
        fwd = wpart(blk(OFF[n], 3), 0, 512)
        send(fwd, fwd, wb_s, wb2_r.at[n, 0], b_next)
        on_chip(n, 1)
        wait(mine, wb_r.at[n, 1])
        fwd = wpart(blk(OFF[n], 1), 512, 512)
        send(fwd, fwd, wb_s, wb2_r.at[n, 1], b_prev)
        on_chip(n, 2)

    def second_axis_end(n):
        wait(wpart(blk(OFF[n], 2), 0, 512), wb2_r.at[n, 0])
        wait(wpart(blk(OFF[n], 2), 512, 512), wb2_r.at[n, 1])
        on_chip(n, 3)

    second_axis(0)

    wait(kv_part(opp, 0), kv2_r.at[0])
    wait(kv_part(opp, 1), kv2_r.at[1])
    send(kv_v.at[opp], kv_v.at[opp], kvc_s.at[3], kvc_r.at[3], other)

    for n in range(3):
        wait(ids_v.at[:, pl.ds(icol, TOK)], sm_r.at[n])
        wait(gat_v.at[:, pl.ds(icol, TOK)], sm_r.at[3 + n])
    ids = ids_v[...]
    gates = gat_v[...]
    mine_ids = NP * z + lax.broadcasted_iota(jnp.int32, (NP, TOKS), 0)
    member = jnp.zeros((NP, TOKS), F32)
    gate_of = jnp.zeros((NP, TOKS), F32)
    for k in range(8):
        hit = ids[k : k + 1, :] == mine_ids
        member = jnp.where(hit, 1.0, member)
        gate_of = jnp.where(hit, gates[k : k + 1, :], gate_of)
    before = (
        lax.broadcasted_iota(jnp.int32, (TOK, TOK), 0) < lax.broadcasted_iota(jnp.int32, (TOK, TOK), 1)
    ).astype(BF)
    places = []
    for n in range(NBLK):
        mb = member[:, n * TOK : (n + 1) * TOK]
        rank = jnp.dot(mb.astype(BF), before, preferred_element_type=F32)
        places.append(jnp.where(mb > 0.5, rank + float(n * CAP), -1.0))
    place = jnp.concatenate(places, axis=1)
    row_id = lax.broadcasted_iota(jnp.int32, (MSG, TOKS), 0).astype(F32)
    for j in range(NP):
        hit = jnp.broadcast_to(place[j : j + 1, :], (MSG, TOKS)) == row_id
        p_v[j * MSG : (j + 1) * MSG, :] = jnp.where(hit, 1.0, 0.0).astype(BF)
        gt_v[j * MSG : (j + 1) * MSG, :] = jnp.where(
            hit, jnp.broadcast_to(gate_of[j : j + 1, :], (MSG, TOKS)), 0.0
        )
    for j in range(ROWS // 128):
        g_v[:, j * 128 : (j + 1) * 128] = gt_v[j * 128 : (j + 1) * 128, :].T.astype(BF)

    second_axis(1)
    for n in range(4):
        wait(own_kv, kvc_r.at[n])
    wait(q_v, loc.at[3])
    softmax_scale = 1.0 / math.sqrt(HEAD)
    allowed = lax.broadcasted_iota(jnp.int32, (2 * TOK, 8 * TOK), 1) <= (
        s * TOK + rem(lax.broadcasted_iota(jnp.int32, (2 * TOK, 8 * TOK), 0), TOK)
    )

    def heads_pair(i, carry):
        g = div(i, 4)
        lane = m8(i * 256, 256)
        kl = m8(g * HEAD, HEAD)
        qq = jnp.concatenate(
            [q_v[:, pl.ds(lane, HEAD)], q_v[:, pl.ds(m8(lane + HEAD, HEAD), HEAD)]], axis=0
        )
        kk = kv_v[:, 0, :, pl.ds(kl, HEAD)].reshape(8 * TOK, HEAD)
        vv = kv_v[:, 1, :, pl.ds(kl, HEAD)].reshape(8 * TOK, HEAD)
        sc = lax.dot_general(qq, kk, (((1,), (1,)), ((), ())), preferred_element_type=F32)
        sc = jnp.where(allowed, sc * softmax_scale, -1e30)
        top = jnp.max(sc, axis=1, keepdims=True)
        p = jnp.exp(sc - top)
        tot = jnp.sum(p, axis=1, keepdims=True)
        o = jnp.dot(p.astype(BF), vv, preferred_element_type=F32) / tot
        o = o.astype(BF)
        attn_v[:, pl.ds(lane, HEAD)] = o[:TOK]
        attn_v[:, pl.ds(m8(lane + HEAD, HEAD), HEAD)] = o[TOK:]
        return carry

    for grp in range(4):
        lax.fori_loop(2 * grp, 2 * grp + 2, heads_pair, 0)
        if grp == 0:
            second_axis(2)
        if grp == 1:
            second_axis_end(0)
            second_axis(3)
        if grp == 2:
            second_axis_end(1)

    my_row = m8(t * HALF_TOK, HALF_TOK)
    their_row = m8((1 - t) * HALF_TOK, HALF_TOK)

    def project(n, m):
        i = blk(OFF[n], OFF[m])
        if n + m > 0:
            wait(mine, wc_r.at[m, n])
        ph_v[i] = jnp.dot(attn_v[...], w_v[i], preferred_element_type=F32).astype(BF)
        send(ph_v.at[i, pl.ds(their_row, HALF_TOK), :], px_v.at[i], px_s, px_r, partner)

    for n in range(3):
        for m in range(3):
            project(n, m)
    project(3, 0)
    project(0, 3)
    project(1, 3)
    project(3, 1)
    second_axis_end(2)
    project(2, 3)
    project(3, 2)
    second_axis_end(3)
    project(3, 3)
    swap(0, 2)
    wait(x_v, loc.at[4])
    wait(gain_v.at[:, pl.ds(gcol, HALF_D)], sm_r.at[6])
    wait(px_v, px_r)
    power = jnp.zeros((HALF_TOK, 1), F32)
    for i in range(NP):
        mix = (
            x_v[pl.ds(my_row, HALF_TOK), i * 128 : (i + 1) * 128].astype(F32)
            + ph_v[i, pl.ds(my_row, HALF_TOK), :].astype(F32)
            + px_v[i].astype(F32)
        )
        mix_v[:, i * 128 : (i + 1) * 128] = mix
        power = power + jnp.sum(mix * mix, axis=1, keepdims=True)
    inverse = lax.rsqrt(power / D + 1e-06)

    zrow = m8(z * HALF_TOK, HALF_TOK)
    def cols_of(f):
        return pl.ds(CS[f], CW[f])

    def ring_open(f):
        cols = cols_of(f)
        xg_v[pl.ds(zrow, HALF_TOK), cols] = (mix_v[:, cols] * inverse * gain_v[:, cols]).astype(BF)
        shard = xg_v.at[pl.ds(zrow, HALF_TOK), cols]
        send(shard, shard, xg_s.at[f, 0], xg_r.at[f, 0, 0], z_next)
        send(shard, shard, xg_s.at[f, 1], xg_r.at[f, 1, 0], z_prev)

    def reach(f, d):
        return 4 if (f + d) % 2 == 0 else 3

    def ring_step(f, k):
        for d in range(2):
            if k > reach(f, d):
                continue
            src_z = zmod(z - k) if d == 0 else zmod(z + k)
            shard = xg_v.at[pl.ds(m8(src_z * HALF_TOK, HALF_TOK), HALF_TOK), cols_of(f)]
            wait(shard, xg_r.at[f, d, k - 1])
            if k + 1 <= reach(f, d):
                send(shard, shard, xg_s.at[f, d], xg_r.at[f, d, k], z_next if d == 0 else z_prev)

    my_slot = pl.ds(m8(e * MSG, 16), MSG)

    def exchange(buf, dst, cols, ss, rs, ls, lo, hi):
        def one(k, carry):
            peer = plane_peer(k)
            send(
                buf.at[pl.ds(m8(peer * MSG, 16), MSG), cols],
                dst.at[my_slot, cols],
                ss,
                rs,
                dev(z, peer, c),
            )
            return carry

        parts = hi - lo + 1
        for n in range(parts):
            lax.fori_loop(1 + n * (NP - 1) // parts, 1 + (n + 1) * (NP - 1) // parts, one, 0)
            if n < parts - 1:
                swap(lo + n, lo + n + 1)
        local(buf.at[my_slot, cols], dst.at[my_slot, cols], ls)

    FIFTEEN = pl.ds(0, (NP - 1) * MSG)

    def exchanged(dst, cols, rs, ls):
        wait(dst.at[FIFTEEN, cols], rs)
        wait(dst.at[my_slot, cols], ls)

    def pick_rows(f):
        cols = cols_of(f)

        def group(i, carry):
            rows = pl.ds(m8(i * 256, 256), 256)
            s_v[rows, cols] = jnp.dot(p_v[rows, :], xg_v[:, cols], preferred_element_type=F32).astype(BF)
            return carry

        lax.fori_loop(0, ROWS // 256, group, 0)
        lo, hi = ((2, 4), (4, 8), (8, 12), (12, GU), (GU, GU + 3))[f]
        exchange(s_v, r_v, cols, dsp_s.at[f], dsp_r.at[f], dsp_l.at[f], lo, hi)

    ring_open(0)
    ring_open(1)
    for wave in range(1, NF + 4):
        for f in range(NF):
            if 1 <= wave - f <= 4:
                ring_step(f, wave - f)
        if wave + 1 < NF:
            ring_open(wave + 1)
        if wave >= 4:
            pick_rows(wave - 4)
    mid = ph_v.at[pl.ds((1 - t) * 8, 8), pl.ds(my_row, HALF_TOK), :]
    send(mid, px2_v, px2_s, px2_r, partner)

    wait(wg_v.at[:, pl.ds(hcol, FFH)], hk.at[0])
    wait(wu_v.at[:, pl.ds(hcol, FFH)], hk.at[1])
    for f in range(NF):
        for n in range(2 * (CS[f] // PIECE), 2 * ((CS[f] + CW[f]) // PIECE)):
            weights_in(n)
        exchanged(r_v, cols_of(f), dsp_r.at[f], dsp_l.at[f])
        lo, hi = CS[f], CS[f] + CW[f]

        def gate_up(i, carry):
            rows = pl.ds(m8(i * 256, 256), 256)
            rr = r_v[rows, lo:hi]
            ga = jnp.dot(rr, wg_v[lo:hi, :], preferred_element_type=F32)
            ua = jnp.dot(rr, wu_v[lo:hi, :], preferred_element_type=F32)
            if f > 0:
                ga = ga + ag_v[rows, :]
                ua = ua + au_v[rows, :]
            if f < NF - 1:
                ag_v[rows, :] = ga
                au_v[rows, :] = ua
            else:
                hid_v[rows, :] = (ga / (1.0 + jnp.exp(-ga)) * ua).astype(BF)
            return carry

        lax.fori_loop(0, ROWS // 256, gate_up, 0)

    wait(wd_v.at[pl.ds(hcol, FFH), :], hk.at[2])
    def pair_cols(u, h):
        return pl.ds(h * HALF_D + RS[u], RW[u])

    def down(n):
        u, h = PAIRS[n]
        weights_in(GU + n)
        cols = pair_cols(u, h)

        def group(i, carry):
            rows = pl.ds(m8(i * 256, 256), 256)
            y0 = jnp.dot(hid_v[rows, :FFH], wd_v[:FFH, cols], preferred_element_type=F32)
            y1 = jnp.dot(hid_v[rows, FFH:], wd_v[FFH:, cols], preferred_element_type=F32)
            y_v[rows, cols] = (y0.astype(BF).astype(F32) + y1.astype(BF).astype(F32)).astype(BF)
            return carry

        lax.fori_loop(0, ROWS // 256, group, 0)

    def give_back(n):
        u, h = PAIRS[n]
        lo = GU + n + 3
        hi = min(lo + 1, SWAPS)
        lo = min(lo, hi)
        exchange(y_v, yr_v, pair_cols(u, h), ret_s.at[u, h], ret_r.at[u, h], ret_l.at[u, h], lo, hi)

    down(0)
    give_back(0)
    down(1)
    give_back(1)
    down(2)
    give_back(2)

    wait(px2_v, px2_r)
    mixo_v[pl.ds(my_row, HALF_TOK), :] = mix_v[:, pl.ds(gcol, HALF_D)]
    for i in range(8):
        cols = pl.ds(m8(gcol + i * 128, 128), 128)
        mixo_v[pl.ds(their_row, HALF_TOK), i * 128 : (i + 1) * 128] = (
            x_v[pl.ds(their_row, HALF_TOK), cols].astype(F32)
            + ph_v[t * 8 + i, pl.ds(their_row, HALF_TOK), :].astype(F32)
            + px2_v[i].astype(F32)
        )

    def combine(u, h):
        cols = pair_cols(u, h)

        def group(i, carry):
            rows = pl.ds(m8(i * 256, 256), 256)
            o_v[rows, cols] = jnp.dot(g_v[rows, :], yr_v[:, cols], preferred_element_type=F32)
            return carry

        lax.fori_loop(0, TOKS // 256, group, 0)

    def own_part(dest, u):
        cols = pl.ds(m8(rem(dest, 2) * HALF_D + RS[u], 128), RW[u])
        return o_v[pl.ds(m8(div(dest, 2) * TOK, TOK), TOK), cols]

    def far(u, d):
        return 4 if (u + d) % 2 == 0 else 3

    def sum_step(u, i):
        cols = pl.ds(RS[u], RW[u])
        for d in range(2):
            dist = far(u, d) - i
            if dist < 1:
                continue
            dest = zmod(z + dist) if d == 0 else zmod(z - dist)
            part = own_part(dest, u)
            if i > 0:
                wait(rs_r.at[d, dist, :, cols], rs_rs.at[u, d, dist])
                part = part + rs_r[d, dist, :, cols].astype(F32)
            rs_s[d, dist - 1, :, cols] = part.astype(BF)
            send(
                rs_s.at[d, dist - 1, :, cols],
                rs_r.at[d, dist - 1, :, cols],
                rs_ss.at[u, d, dist - 1],
                rs_rs.at[u, d, dist - 1],
                z_next if d == 0 else z_prev,
            )

    FAR_FIRST = (4, 3, 5, 2, 6, 1, 7)

    def send_sums(u):
        for k in FAR_FIRST:
            dest = zmod(z + k)
            ds_v[u - RING_U, k - 1] = own_part(dest, u).astype(BF)
            send(
                ds_v.at[u - RING_U, k - 1],
                dr_v.at[u - RING_U, k - 1],
                ds_s.at[u - RING_U],
                ds_r.at[u - RING_U],
                dev(dest, e, c),
            )

    def finish(u):
        cols = pl.ds(RS[u], RW[u])
        total = own_part(z, u)
        if u < RING_U:
            for d in range(2):
                wait(rs_r.at[d, 0, :, cols], rs_rs.at[u, d, 0])
                total = total + rs_r[d, 0, :, cols].astype(F32)
        else:
            wait(dr_v.at[u - RING_U], ds_r.at[u - RING_U])
            for k in range(NZ - 1):
                total = total + dr_v[u - RING_U, k].astype(F32)
        out_ref[:, cols] = (mixo_v[:, cols] + total).astype(BF)

    last = 2 * NU
    for n in range(2, last + 5):
        for u in reversed(range(NU)):
            i = n - (2 * u + 4)
            if u >= RING_U:
                if i == 0:
                    send_sums(u)
            elif 0 <= i < 4:
                sum_step(u, i)
            elif i == 4:
                finish(u)
        if n + 1 < last:
            down(n + 1)
        if n - 2 < last:
            u, h = PAIRS[n - 2]
            exchanged(yr_v, pair_cols(u, h), ret_r.at[u, h], ret_l.at[u, h])
        if n + 1 < last:
            give_back(n + 1)
        if n - 2 < last:
            combine(*PAIRS[n - 2])
    for u in range(RING_U, NU):
        finish(u)

    for n in range(2):
        for d in range(2):
            wait(kv_part(s, n), kv_s.at[d, n])
        wait(kv_part(s, n), kv2_s.at[n])
    for n in range(4):
        wait(own_kv, kvc_s.at[n])
    for n in range(3):
        wait(ids_v.at[:, pl.ds(0, TOK)], sm_s.at[n])
        wait(gat_v.at[:, pl.ds(0, TOK)], sm_s.at[3 + n])
    wait(gain_mine, sm_s.at[6])
    wait(w_v.at[pl.ds(0, 3), pl.ds(0, WROWS), :], wa_s)
    wait(w_v.at[pl.ds(0, 12), pl.ds(0, WROWS), :], wb_s)
    wait(w_v.at[pl.ds(0, 15), pl.ds(0, WROWS), :], wc_s)
    wait(px_v, px_s)
    for f in range(NF):
        wait(s_v.at[FIFTEEN, cols_of(f)], dsp_s.at[f])
        for d in range(2):
            wait(xg_v.at[pl.ds(0, reach(f, d) * HALF_TOK), cols_of(f)], xg_s.at[f, d])
    wait(px2_v, px2_s)
    for u in range(NU):
        for h in range(2):
            wait(y_v.at[FIFTEEN, pair_cols(u, h)], ret_s.at[u, h])
        for d in range(2):
            for n in range(far(u, d) if u < RING_U else 0):
                wait(rs_s.at[d, n, :, pl.ds(RS[u], RW[u])], rs_ss.at[u, d, n])
        if u >= RING_U:
            wait(ds_v.at[u - RING_U], ds_s.at[u - RING_U])

    @pl.when(giver == 0)
    def _():
        wait(wg_h, wk_s.at[0])
        wait(wu_h, wk_s.at[1])
        wait(wd_h, wk_s.at[2])

    @pl.when(giver == 1)
    def _():
        for n in range(SWAPS):
            wait(mine_chunks[n][1], wz_s.at[n])
            wait(mine_chunks[n][1], wf_s.at[n])


def per_device(
    q_rows, k_rows, value_rows, x_rows, out_weight, norm_gain, w_gate, w_up, w_down, expert_ids, gate_weights
):
    dma = pltpu.SemaphoreType.DMA
    any_spec = pl.BlockSpec(memory_space=pl.ANY)
    out = pl.pallas_call(
        layer_kernel,
        out_shape=jax.ShapeDtypeStruct((TOK, HALF_D), BF),
        in_specs=[any_spec] * 11,
        out_specs=pl.BlockSpec(memory_space=pltpu.VMEM),
        scratch_shapes=[
            pltpu.VMEM((TOK, D), BF),
            pltpu.VMEM((TOK, D), BF),
            pltpu.VMEM((8, 2, TOK, 256), BF),
            pltpu.VMEM((NP, D, 128), BF),
            pltpu.VMEM((1, D), F32),
            pltpu.VMEM((8, TOKS), jnp.int32),
            pltpu.VMEM((8, TOKS), F32),
            pltpu.VMEM((TOK, D), BF),
            pltpu.VMEM((NP, TOK, 128), BF),
            pltpu.VMEM((NP, HALF_TOK, 128), BF),
            pltpu.VMEM((8, HALF_TOK, 128), BF),
            pltpu.VMEM((HALF_TOK, D), F32),
            pltpu.VMEM((TOK, HALF_D), F32),
            pltpu.VMEM((TOKS, D), BF),
            pltpu.VMEM((ROWS, TOKS), BF),
            pltpu.VMEM((ROWS, TOKS), F32),
            pltpu.VMEM((TOKS, ROWS), BF),
            pltpu.VMEM((ROWS, D), BF),
            pltpu.VMEM((ROWS, D), BF),
            pltpu.VMEM((D, FF), BF),
            pltpu.VMEM((D, FF), BF),
            pltpu.VMEM((FF, D), BF),
            pltpu.VMEM((ROWS, FF), F32),
            pltpu.VMEM((ROWS, FF), F32),
            pltpu.VMEM((ROWS, FF), BF),
            pltpu.VMEM((ROWS, D), BF),
            pltpu.VMEM((ROWS, D), BF),
            pltpu.VMEM((TOKS, D), F32),
            pltpu.VMEM((2, 4, TOK, HALF_D), BF),
            pltpu.VMEM((2, 4, TOK, HALF_D), BF),
            pltpu.VMEM((NU - RING_U, NZ - 1, TOK, 128), BF),
            pltpu.VMEM((NU - RING_U, NZ - 1, TOK, 128), BF),
            dma((8,)), dma((3,)), dma((SWAPS,)), dma((SWAPS,)), dma((3,)), dma((SWAPS,)),
            dma((2, 2)), dma((2, 2)), dma((4,)), dma((4,)), dma((2,)), dma((2,)),
            dma((7,)), dma((7,)),
            dma, dma((2,)), dma((2,)), dma, dma((4, 2)), dma((4, 2)), dma, dma((4, 4)),
            dma, dma, dma, dma,
            dma((NF, 2)), dma((NF, 2, 4)), dma((NF,)), dma((NF,)), dma((NF,)),
            dma((NU, 2)), dma((NU, 2)), dma((NU, 2)),
            dma((NU, 2, 4)), dma((NU, 2, 4)), dma((NU - RING_U,)), dma((NU - RING_U,)),
        ],
        compiler_params=pltpu.CompilerParams(
            collective_id=0, has_side_effects=True, vmem_limit_bytes=62 * 1024 * 1024
        ),
        name="layer",
    )(
        q_rows[0],
        k_rows[0],
        value_rows[0],
        x_rows[0],
        out_weight,
        norm_gain.reshape(1, HALF_D),
        w_gate[0],
        w_up[0],
        w_down[0],
        expert_ids[0].T,
        gate_weights[0].T,
    )
    return out[None]


def solution(mesh):
    return jax.shard_map(
        per_device,
        mesh=mesh,
        in_specs=(
            P("expert", "seq", "tensor"),
            P("expert", "seq", "tensor"),
            P("expert", "seq", "tensor"),
            P("expert", "seq", None),
            P("tensor", "expert"),
            P("tensor"),
            P(("seq", "expert"), None, "tensor"),
            P(("seq", "expert"), None, "tensor"),
            P(("seq", "expert"), "tensor", None),
            P("expert", "seq", None),
            P("expert", "seq", None),
        ),
        out_specs=P("expert", "seq", "tensor"),
        check_vma=False,
    )
```
